512 devices in a mesh: row: 32 (over y, x), col: 16 (over z, core).
Axes of the slice: x: 4, y: 8, z: 8, core: 2. Of those that a mesh axis runs over, the one named last changes fastest.
Arguments:
- atom_types: int32 [512, 256], P(('row', 'col')), may hold values from 0 to 3
- neighbor_ids: int32 [512, 32, 256], P(('row', 'col')), may hold values from 0 to 255
- switching: float32 [512, 32, 256], P(('row', 'col')), may hold values from 0.1 to 1
- environment: float32 [512, 256, 64], P(('row', 'col')), may hold values from -6 to 6
- force_weights: float32 [512, 256], P(('row', 'col')), may hold values from -1 to 1
- targets: float32 [512], P(('row', 'col')), may hold values from -6 to 6
- type_embed: float32 [4, 64], replicated, may hold values from -8 to 8, as said below
- layer_weight: float32 [64, 128], replicated, may hold values from -1 to 1
- out_weight: float32 [128], replicated, may hold values from -0.5 to 0.5
- covariance: float32 [8192, 8192], P('row', 'col'), as said below
Outputs:
- new_weight: float32 [8192], P(('row', 'col'))
- new_cov: float32 [8192, 8192], P('row', 'col')
The draws below stay inside these ranges and needn't reach their ends.
Inputs may be any that keep to these rules, and one draw needn't show every extreme that they name: `neighbor_ids`: indices of atoms of the same configuration. `covariance`: symmetric positive definite. `type_embed`: each feature sums to zero over the 4 types.
All inputs are finite; a program needn't handle non-finite values. Where the reference program divides by a largest or mean magnitude, that divisor is 1e-20 or more.
Results may differ from the reference program's by a relative error of at most 0.0003.
Values sent between devices are 32-bit elements; how exact they have to be, the bound alone decides.
A program may use at most 64 MiB of HBM per device.

```python
import math
import jax
import jax.numpy as jnp
from jax import lax

H = 128
HIN = 64
TYPES = 4
NBR = 32
NEWTON = 4
ATOMS = 256
NPARAM = 8192
STREAMS = 512


def draw_covariance(key, part):
    keys = jax.random.split(jax.random.fold_in(key, 11), 5)
    noise = jax.random.normal(keys[0], (NPARAM, NPARAM), jnp.float32)
    symmetric = (noise + noise.T) * (0.3 / math.sqrt(NPARAM))
    diagonal = jax.random.uniform(keys[1], (NPARAM,), jnp.float32, 1.0, 2.0)
    input_factor = jax.random.normal(keys[3], (HIN, HIN), jnp.float32)
    output_factor = jax.random.normal(keys[4], (H, H), jnp.float32)
    input_corr = jnp.dot(input_factor, input_factor.T, precision=jax.lax.Precision.HIGHEST) / HIN
    output_corr = jnp.dot(output_factor, output_factor.T, precision=jax.lax.Precision.HIGHEST) / H
    coupled = (input_corr[:, None, :, None] * output_corr[None, :, None, :]).reshape(NPARAM, NPARAM)
    matrix = symmetric + jnp.diag(diagonal) + coupled
    return matrix


def draw_environment(key, part):
    inner = jax.random.fold_in(key, 23)
    values = jnp.clip(jax.random.normal(inner, (STREAMS, ATOMS, HIN), jnp.float32), -6.0, 6.0)
    return values


def draw_force_weights(key, part):
    inner = jax.random.fold_in(key, 37)
    values = jax.random.uniform(inner, (STREAMS, ATOMS), jnp.float32, -1.0, 1.0)
    return values


def draw_type_embed(key, part):
    inner = jax.random.fold_in(key, 41)
    values = jnp.clip(jax.random.normal(inner, (TYPES, HIN), jnp.float32), -4.0, 4.0)
    return values - jnp.mean(values, axis=0, keepdims=True)


def draw_layer_weight(key, part):
    inner = jax.random.fold_in(key, 53)
    spread = 3.0 / math.sqrt(HIN)
    values = jax.random.normal(inner, (HIN, H), jnp.float32) * spread
    return jnp.clip(values, -1.0, 1.0)


def with_ends(result, key, low, high):
    spot = [jax.random.randint(jax.random.fold_in(key, axis), (), 0, length) for axis, length in enumerate(result.shape)]
    widest = result.shape.index(max(result.shape))
    neighbour = spot[:widest] + [(spot[widest] + 1) % result.shape[widest]] + spot[widest + 1:]
    return result.at[tuple(spot)].set(low).at[tuple(neighbour)].set(high)


def level_of(own_key, shape, pieces, low, largest):
    factor_of, own = 1.0, jax.random.fold_in(own_key, 6)
    for axis_at, parts in pieces:
        draws = jnp.exp(jax.random.uniform(jax.random.fold_in(own, axis_at), (parts,), jnp.float32, low / len(pieces), largest / len(pieces)))
        factor_of = factor_of * jnp.repeat(draws, shape[axis_at] // parts).reshape([-1 if axis == axis_at else 1 for axis in range(len(shape))])
    return factor_of


def scatter_about(stream_key, shape, scale, limit, cuts=(), kind=jnp.bfloat16):
    level = level_of(stream_key, shape, cuts, -0.22, 0.18) if cuts else 1.0
    result = jax.random.normal(stream_key, shape, jnp.float32) * scale * level
    return jnp.minimum(jnp.maximum(result, -limit), limit).astype(kind)


def setup_inputs(seed: int = 0) -> dict:
    seeds = jax.random.split(jax.random.key(seed), 11)
    atom_types = with_ends(jax.random.randint(seeds[0], (STREAMS, ATOMS), 0, TYPES), jax.random.fold_in(seeds[0], 1), 0, TYPES - 1).astype(jnp.int32)
    neighbor_ids = with_ends(jax.random.randint(seeds[1], (STREAMS, NBR, ATOMS), 0, ATOMS), jax.random.fold_in(seeds[1], 1), 0, ATOMS - 1).astype(jnp.int32)
    switching = jnp.clip(0.1 + 0.9 * jax.random.uniform(seeds[2], (STREAMS, NBR, ATOMS), jnp.float32) ** level_of(seeds[2], (STREAMS, NBR, ATOMS), ((0, 512),), -0.2, 0.2), 0.1, 1.0)
    environment = draw_environment(jax.random.fold_in(seeds[10], 71), 0)
    force_weights = draw_force_weights(jax.random.fold_in(seeds[10], 71), 0)
    targets = scatter_about(seeds[5], (STREAMS,), 1.0, 6.0, ((0, 512),), jnp.float32)
    type_embed = draw_type_embed(jax.random.fold_in(seeds[10], 71), 0)
    layer_weight = draw_layer_weight(jax.random.fold_in(seeds[10], 71), 0)
    out_weight = scatter_about(seeds[8], (H,), H ** -0.5, 0.5, (), jnp.float32)
    covariance = draw_covariance(jax.random.fold_in(seeds[10], 71), 0)
    return dict(atom_types=atom_types, neighbor_ids=neighbor_ids, switching=switching, environment=environment, force_weights=force_weights, targets=targets, type_embed=type_embed, layer_weight=layer_weight, out_weight=out_weight, covariance=covariance)


forget = 0.98
highest = lax.Precision.HIGHEST

def network(atom_types, neighbor_ids, switching, environment, force_weights, type_embed, layer_weight, out_weight):
    type_ids = jnp.arange(type_embed.shape[0], dtype=jnp.int32)
    onehot = (atom_types[:, None] == type_ids[None, :]).astype(jnp.float32)
    mixed = environment + jnp.dot(onehot, type_embed, precision=highest)
    nearby = jnp.take(mixed, neighbor_ids, axis=0)
    descriptor = lax.optimization_barrier(jnp.sum(switching[:, :, None] * nearby, axis=0)) / math.sqrt(neighbor_ids.shape[0])
    hidden = jnp.tanh(descriptor)
    activity = jnp.tanh(jnp.dot(hidden, layer_weight, precision=highest))
    energy = jnp.dot(activity, out_weight, precision=highest)
    atom_scale = 1.0 / math.sqrt(energy.shape[0])
    predicted = jnp.sum(force_weights * energy) * atom_scale
    slopes = out_weight[None, :] * (1.0 - activity * activity)
    jacobian = jnp.dot((force_weights[:, None] * hidden).T, slopes, precision=highest) * atom_scale
    return (predicted, jacobian.reshape(-1))

def first_inverse(innovation):
    identity = jnp.eye(innovation.shape[0], dtype=jnp.float32)
    row_bound = jnp.max(lax.optimization_barrier(jnp.sum(jnp.abs(innovation), axis=1)))
    return identity * (2.0 / row_bound) - innovation / (row_bound * row_bound)

def reference(atom_types, neighbor_ids, switching, environment, force_weights, targets, type_embed, layer_weight, out_weight, covariance):

    def single(inputs):
        return network(inputs[0], inputs[1], inputs[2], inputs[3], inputs[4], type_embed, layer_weight, out_weight)
    predicted, jacobian = lax.map(single, (atom_types, neighbor_ids, switching, environment, force_weights))
    errors = targets - predicted
    cross = jnp.dot(covariance, jacobian.T, precision=highest)
    identity = jnp.eye(jacobian.shape[0], dtype=jnp.float32)
    innovation = jnp.dot(jacobian, cross, precision=highest) + forget * identity
    inverse = first_inverse(innovation)
    for repeat in range(NEWTON - 1):
        inverse = 2.0 * inverse - jnp.dot(jnp.dot(inverse, innovation, precision=highest), inverse, precision=highest)
    gain = jnp.dot(cross, inverse, precision=highest)
    new_weight = layer_weight.reshape(-1) + jnp.dot(gain, errors, precision=highest)
    new_cov = (covariance - jnp.dot(gain, cross.T, precision=highest)) / forget
    return (new_weight, new_cov)
```

```python
import functools
import math

import jax
import jax.numpy as jnp
from jax import lax
from jax.experimental import pallas as pl
from jax.experimental.pallas import tpu as pltpu
from jax.sharding import PartitionSpec as P

FORGET = 0.98
MESH = pl.DeviceIdType.MESH
F32 = jnp.float32
BF16 = jnp.bfloat16
NX, NY, NZ = 4, 8, 8
NR, NC = 32, 16


def split(a):
    hi = a.astype(BF16)
    lo = (a - hi.astype(F32)).astype(BF16)
    return hi, lo


def mm(a, b, dims):
    return lax.dot_general(a, b, (dims, ((), ())), preferred_element_type=F32)


def dot3(a, b, dims):
    ah, al = a if isinstance(a, tuple) else split(a)
    bh, bl = b if isinstance(b, tuple) else split(b)
    return mm(ah, bh, dims) + (mm(ah, bl, dims) + mm(al, bh, dims))


ROWS = ((1,), (1,))
COLS = ((0,), (0,))
NORMAL = ((1,), (0,))


def kernel(
    types_ref, nbr_ref, sw_ref, env_ref, fw_ref, tgt_ref, te_ref, w_ref, ow_ref, cov_ref,
    newcov_ref, delta_ref,
    select, jrow_send, jcol_send, e_send, jr_recv, jc_recv, e_recv, e_all,
    jr_all, jc_all, w_send, w_recv, art,
    w2_send, x_recv, y_send, y_recv, act,
    s_send, s_recv, s_row, s_all,
    send, recv, jc_y, act_y, s_z,
):
    r = lax.axis_index("row")
    c = lax.axis_index("col")
    x, y = lax.rem(r, NX), lax.div(r, NX)
    k, z = lax.rem(c, 2), lax.div(c, 2)

    def row_peer(j):
        return lax.rem(r + j, NR)

    def col_peer(j):
        return lax.rem(c + j, NC)

    def x_peer(j):
        return y * NX + lax.rem(x + j, NX)

    def y_peer(j):
        return lax.rem(y + j, NY) * NX + x

    def z_peer(j):
        return lax.rem(z + j, NZ) * 2 + k

    def push(src, dst, send_sem, recv_sem, **where):
        pltpu.make_async_remote_copy(
            src_ref=src, dst_ref=dst, send_sem=send_sem, recv_sem=recv_sem,
            device_id=where, device_id_type=MESH,
        ).start()

    def settle(ref, sem):
        pltpu.make_async_copy(ref, ref, sem).wait()

    barrier = pltpu.get_barrier_semaphore()

    @pl.loop(1, NR)
    def _(j):
        pl.semaphore_signal(barrier, inc=1, device_id={"row": row_peer(j)}, device_id_type=MESH)

    @pl.loop(1, NC)
    def _(j):
        pl.semaphore_signal(barrier, inc=1, device_id={"col": col_peer(j)}, device_id_type=MESH)

    block = 32

    @pl.loop(0, 256 // block)
    def _(b):
        ids = lax.broadcasted_iota(jnp.int32, (block, 256), 0) + b * block
        total = jnp.zeros((block, 256), F32)
        for n in range(32):
            total += jnp.where(ids == nbr_ref[n : n + 1, :], sw_ref[n : n + 1, :], 0.0)
        select[pl.ds(b * block, block), :] = total

    kinds = lax.broadcasted_iota(jnp.int32, (4, 256), 0)
    onehot = (kinds == types_ref[...]).astype(F32)
    mixed = env_ref[...] + dot3(onehot, te_ref[...], COLS)
    descriptor = dot3(mixed, select[...], COLS) / math.sqrt(32)
    hidden = jnp.tanh(descriptor)
    activity = jnp.tanh(dot3(hidden, w_ref[...], COLS))
    weighted = dot3(fw_ref[...], activity, NORMAL)
    scale = 1.0 / math.sqrt(256)
    predicted = jnp.sum(weighted * ow_ref[...], axis=1, keepdims=True) * scale
    error = tgt_ref[...] - predicted
    slopes = ow_ref[...] * (1.0 - activity * activity)
    jac = dot3(hidden * fw_ref[...], slopes, NORMAL) * scale

    for n in range(NR):
        jrow_send[n] = jac[2 * n : 2 * n + 2, :]
    for n in range(NC):
        jcol_send[n] = jac[4 * n : 4 * n + 4, :]
    e_send[0] = jnp.broadcast_to(error, (1, 128))

    pl.semaphore_wait(barrier, NR - 1 + NC - 1)

    @pl.loop(1, NC)
    def _(j):
        p = col_peer(j)
        push(jcol_send.at[p], jc_recv.at[c], send.at[0], recv.at[0], col=p)

    @pl.loop(1, NR)
    def _(j):
        p = row_peer(j)
        push(jrow_send.at[p], jr_recv.at[r], send.at[1], recv.at[1], row=p)
        push(e_send.at[0], e_recv.at[r], send.at[2], recv.at[2], row=p)

    jc_recv[c] = jcol_send[c]
    jr_recv[r] = jrow_send[r]
    e_recv[r] = e_send[0]

    settle(jc_recv.at[pl.ds(0, NC - 1)], recv.at[0])
    jc_all[r] = jnp.concatenate([jc_recv[:, n, :] for n in range(4)], axis=1)

    def gather_y(buf, sem, first, sems):
        for j in (1, 7, 2, 6, 3, 5, 4):
            push(buf.at[r], buf.at[r], send.at[first], sems.at[j], row=y_peer(j))
        for i in (1, 3, 2):
            push(buf.at[r], buf.at[r], send.at[first + 1], recv.at[sem], row=x_peer(i))

    def gather_x(buf, sem, first, sems):
        for j in (1, 7, 2, 6, 3, 5, 4):
            slot = y_peer(NY - j)
            settle(buf.at[slot], sems.at[j])
            for i in (1, 3, 2):
                push(buf.at[slot], buf.at[slot], send.at[first + 1], recv.at[sem], row=x_peer(i))

    gather_y(jc_all, 3, 3, jc_y)

    settle(jr_recv.at[pl.ds(0, NR - 1)], recv.at[1])
    jr_all[c] = jnp.concatenate([jr_recv[:, n, :] for n in range(2)], axis=1)
    settle(e_recv.at[pl.ds(0, NR - 1)], recv.at[2])
    lanes = lax.broadcasted_iota(jnp.int32, (NR, 128), 1)
    spots = lax.broadcasted_iota(jnp.int32, (NR, 128), 0)
    e_all[c] = jnp.sum(jnp.where(lanes == spots, e_recv[:, 0, :], 0.0), axis=0, keepdims=True)

    @pl.loop(1, NC)
    def _(j):
        p = col_peer(j)
        push(jr_all.at[c], jr_all.at[c], send.at[5], recv.at[4], col=p)
        push(e_all.at[c], e_all.at[c], send.at[6], recv.at[5], col=p)

    gather_x(jc_all, 3, 3, jc_y)
    settle(jc_all.at[pl.ds(0, NX * NY - NY)], recv.at[3])

    cov = split(cov_ref[...])
    part = dot3(jc_all[...].reshape(512, 512), cov, ROWS)
    at = lax.broadcasted_iota(jnp.int32, (512, 512), 0)
    to = lax.broadcasted_iota(jnp.int32, (512, 512), 1)
    order = (to == lax.rem(at, NR) * NC + lax.div(at, NR)).astype(F32).astype(BF16)
    ph, plow = split(part)
    part = mm(order, ph, NORMAL) + mm(order, plow, NORMAL)
    w_send[...] = part.reshape(NC, NR, 256)

    @pl.loop(1, NC)
    def _(j):
        p = col_peer(j)
        push(w_send.at[p], w_recv.at[c], send.at[7], recv.at[6], col=p)

    w_recv[c] = w_send[c]

    settle(jr_all.at[pl.ds(0, NC - 1)], recv.at[4])
    jr = split(jr_all[...].reshape(512, 256))
    w2_send[...] = dot3(jr, cov, NORMAL).reshape(NY, NX, 16, 512)
    for i in (1, 3, 2):
        px = lax.rem(x + i, NX)
        push(w2_send.at[:, px], x_recv.at[i], send.at[8], recv.at[7], row=x_peer(i))

    settle(w_recv.at[pl.ds(0, NC - 1)], recv.at[6])
    own = jnp.sum(w_recv[...], axis=0)
    art[c] = own
    s_part = dot3(own, jr, ROWS)
    for n in range(4):
        s_send[:, n, :] = s_part[:, 128 * n : 128 * n + 128]

    @pl.loop(1, NR)
    def _(j):
        p = row_peer(j)
        push(s_send.at[p], s_recv.at[r], send.at[9], recv.at[8], row=p)

    s_recv[r] = s_send[r]

    @pl.loop(1, NC)
    def _(j):
        push(art.at[c], art.at[c], send.at[10], recv.at[9], col=col_peer(j))

    settle(s_recv.at[pl.ds(0, NR - 1)], recv.at[8])
    s_row[r] = jnp.sum(s_recv[...], axis=0)

    @pl.loop(1, NR)
    def _(j):
        push(s_row.at[r], s_row.at[r], send.at[11], recv.at[10], row=row_peer(j))

    settle(x_recv.at[pl.ds(1, NX - 1)], recv.at[7])
    y_send[...] = w2_send[:, x] + x_recv[1] + x_recv[2] + x_recv[3]
    for j in (1, 7, 2, 6, 3, 5, 4):
        py = lax.rem(y + j, NY)
        push(y_send.at[py], y_recv.at[j], send.at[12], recv.at[11], row=y_peer(j))

    settle(s_row.at[pl.ds(0, NR - 1)], recv.at[10])
    s_all[c] = jnp.concatenate([s_row[:, n, :] for n in range(4)], axis=1)
    for j in (1, 7, 2, 6, 3, 5, 4):
        push(s_all.at[c], s_all.at[c], send.at[13], s_z.at[j], col=z_peer(j))
    partner = z * 2 + 1 - k
    push(s_all.at[c], s_all.at[c], send.at[14], recv.at[12], col=partner)

    settle(y_recv.at[pl.ds(1, NY - 1)], recv.at[11])
    total = y_send[y]
    for j in range(1, NY):
        total += y_recv[j]
    act[r] = total
    gather_y(act, 13, 15, act_y)

    for j in (1, 7, 2, 6, 3, 5, 4):
        slot = z_peer(NZ - j)
        settle(s_all.at[slot], s_z.at[j])
        push(s_all.at[slot], s_all.at[slot], send.at[14], recv.at[12], col=partner)
    gather_x(act, 13, 15, act_y)
    settle(s_all.at[pl.ds(0, NZ)], recv.at[12])

    eye = at == to
    innovation = s_all[...].reshape(512, 512) + jnp.where(eye, FORGET, 0.0)
    bound = jnp.max(jnp.sum(jnp.abs(innovation), axis=0, keepdims=True), axis=1, keepdims=True)
    settle(art.at[pl.ds(0, NC - 1)], recv.at[9])
    power = split(jnp.where(eye, 1.0, 0.0) - innovation / bound)
    gain = art[...].reshape(512, 256) / bound
    for step in range(4):
        gain = gain + dot3(power, gain, NORMAL)
        if step < 3:
            power = split(dot3(power, power, NORMAL))

    settle(e_all.at[pl.ds(0, NC - 1)], recv.at[5])
    spread = (
        lax.broadcasted_iota(jnp.int32, (512, NC), 1)
        == lax.div(lax.broadcasted_iota(jnp.int32, (512, NC), 0), NR)
    ).astype(F32)
    errors = jnp.concatenate([e_all[n] for n in range(NC)], axis=0)
    picked = jnp.dot(spread, errors, precision=lax.Precision.HIGHEST)
    own_lane = lax.broadcasted_iota(jnp.int32, (512, 128), 1) == lax.rem(
        lax.broadcasted_iota(jnp.int32, (512, 128), 0), NR
    )
    column = jnp.sum(jnp.where(own_lane, picked, 0.0), axis=1, keepdims=True)
    delta_ref[...] = jnp.sum(gain * column, axis=0, keepdims=True)

    settle(act.at[pl.ds(0, NX * NY - NY)], recv.at[13])
    update = dot3(gain, act[...].reshape(512, 512), COLS)
    newcov_ref[...] = (cov_ref[...] - update) * (1.0 / FORGET)

    settle(jcol_send.at[pl.ds(0, NC - 1)], send.at[0])
    settle(jrow_send.at[pl.ds(0, NR - 1)], send.at[1])
    settle(e_recv.at[pl.ds(0, NR - 1)], send.at[2])
    settle(jc_all.at[pl.ds(0, NY - 1)], send.at[3])
    settle(jc_all.at[pl.ds(0, NX * NY - NY)], send.at[4])
    settle(jr_all.at[pl.ds(0, NC - 1)], send.at[5])
    settle(e_all.at[pl.ds(0, NC - 1)], send.at[6])
    settle(w_send.at[pl.ds(0, NC - 1)], send.at[7])
    settle(x_recv.at[pl.ds(1, NX - 1)], send.at[8])
    settle(s_send.at[pl.ds(0, NR - 1)], send.at[9])
    settle(art.at[pl.ds(0, NC - 1)], send.at[10])
    settle(s_row.at[pl.ds(0, NR - 1)], send.at[11])
    settle(y_recv.at[pl.ds(1, NY - 1)], send.at[12])
    settle(s_all.at[pl.ds(0, NZ - 1)], send.at[13])
    settle(s_all.at[pl.ds(0, NZ)], send.at[14])
    settle(act.at[pl.ds(0, NY - 1)], send.at[15])
    settle(act.at[pl.ds(0, NX * NY - NY)], send.at[16])


def on_device(
    atom_types, neighbor_ids, switching, environment, force_weights, targets,
    type_embed, layer_weight, out_weight, covariance,
):
    vmem = pl.BlockSpec(memory_space=pltpu.VMEM)
    V = pltpu.VMEM
    scratch = [
        V((256, 256), F32), V((NR, 2, 128), F32), V((NC, 4, 128), F32), V((1, 1, 128), F32),
        V((NR, 2, 128), F32), V((NC, 4, 128), F32), V((NR, 1, 128), F32), V((NC, 1, 128), F32),
        V((NC, NR, 256), F32), V((NR, NC, 512), F32), V((NC, NR, 256), F32),
        V((NC, NR, 256), F32), V((NC, NR, 256), F32),
        V((NY, NX, 16, 512), F32), V((NX, NY, 16, 512), F32), V((NY, 16, 512), F32),
        V((NY, 16, 512), F32), V((NR, 16, 512), F32),
        V((NR, 4, 128), F32), V((NR, 4, 128), F32), V((NR, 4, 128), F32), V((NC, NR, 512), F32),
        pltpu.SemaphoreType.DMA((17,)), pltpu.SemaphoreType.DMA((14,)),
        pltpu.SemaphoreType.DMA((NY,)), pltpu.SemaphoreType.DMA((NY,)), pltpu.SemaphoreType.DMA((NZ,)),
    ]
    new_cov, delta = pl.pallas_call(
        kernel,
        out_shape=(
            jax.ShapeDtypeStruct((256, 512), F32),
            jax.ShapeDtypeStruct((1, 256), F32),
        ),
        in_specs=[vmem] * 10,
        out_specs=(vmem, vmem),
        scratch_shapes=scratch,
        compiler_params=pltpu.CompilerParams(
            collective_id=0, has_side_effects=True, vmem_limit_bytes=60 * 1024 * 1024
        ),
    )(
        atom_types, neighbor_ids[0], switching[0], environment[0], force_weights,
        targets.reshape(1, 1), type_embed, layer_weight, out_weight.reshape(1, 128), covariance,
    )
    row_at = lax.axis_index("row")
    col_at = lax.axis_index("col")
    flat_weight = layer_weight.reshape(-1)
    own_weight = lax.dynamic_slice_in_dim(flat_weight, (row_at * NC + col_at) * 16, 16, 0)
    new_weight = own_weight + lax.dynamic_slice_in_dim(delta[0], col_at * 16, 16, 0)
    return (new_weight, new_cov)


def solution(mesh):
    in_specs = (
        P(("row", "col"), None),
        P(("row", "col"), None, None),
        P(("row", "col"), None, None),
        P(("row", "col"), None, None),
        P(("row", "col"), None),
        P(("row", "col")),
        P(),
        P(),
        P(),
        P("row", "col"),
    )
    out_specs = (P(("row", "col")), P("row", "col"))
    return jax.shard_map(
        on_device, mesh=mesh, in_specs=in_specs, out_specs=out_specs, check_vma=False
    )
```

```python
import functools
import math

import jax
import jax.numpy as jnp
from jax import lax
from jax.experimental import pallas as pl
from jax.experimental.pallas import tpu as pltpu
from jax.sharding import PartitionSpec as P

FORGET = 0.98
MESH = pl.DeviceIdType.MESH
F32 = jnp.float32
BF16 = jnp.bfloat16
NX, NY, NZ = 4, 8, 8
NR, NC = 32, 16
NEAR = (1, 7, 2, 6, 3, 5, 4)
GROUPS = (
    "jcol", "jrow", "err", "jc_y", "jc_x", "jr_z", "jr_p", "e", "w", "art_z", "art_p",
    "s_x", "s_y", "s_z", "s_g", "s_p", "act_y", "act_x",
)


def split(a):
    hi = a.astype(BF16)
    lo = (a - hi.astype(F32)).astype(BF16)
    return hi, lo


def mm(a, b, dims):
    return lax.dot_general(a, b, (dims, ((), ())), preferred_element_type=F32)


def dot3(a, b, dims):
    ah, al = a if isinstance(a, tuple) else split(a)
    bh, bl = b if isinstance(b, tuple) else split(b)
    return mm(ah, bh, dims) + (mm(ah, bl, dims) + mm(al, bh, dims))


ROWS = ((1,), (1,))
COLS = ((0,), (0,))
NORMAL = ((1,), (0,))


def kernel(
    types_ref, nbr_ref, sw_ref, env_ref, fw_ref, tgt_ref, te_ref, w_ref, ow_ref, cov_ref,
    newcov_ref, weight_ref,
    select, cov_hi, cov_lo, order, jrow_send, jcol_send, e_send, jr_recv, jc_recv, e_recv, e_all,
    jr_all, jc_all, w_send, w_recv, art, turned, act,
    s_send, s_x, s_y, s_all,
    send, recv, jc_y, jc_x, act_y, s_z, s_g, turn_send, turn_recv,
):
    r = lax.axis_index("row")
    c = lax.axis_index("col")
    x, y = lax.rem(r, NX), lax.div(r, NX)
    k, z = lax.rem(c, 2), lax.div(c, 2)

    def row_peer(j):
        return lax.rem(r + j, NR)

    def col_peer(j):
        return lax.rem(c + j, NC)

    def x_peer(j):
        return y * NX + lax.rem(x + j, NX)

    def y_peer(j):
        return lax.rem(y + j, NY) * NX + x

    def z_peer(j):
        return lax.rem(z + j, NZ) * 2 + k

    partner = z * 2 + 1 - k
    flight = {}

    def push(name, src, dst, sem=None, **where):
        at = GROUPS.index(name)
        pltpu.make_async_remote_copy(
            src_ref=src, dst_ref=dst, send_sem=send.at[at],
            recv_sem=recv.at[at] if sem is None else sem,
            device_id=where, device_id_type=MESH,
        ).start()

    def settle(ref, sem):
        pltpu.make_async_copy(ref, ref, sem).wait()

    def track(name, sent, got=None):
        at = GROUPS.index(name)
        flight[name] = [(sent, send.at[at])]
        if got is not None:
            flight[name].append((got, recv.at[at]))

    def land(name):
        settle(*flight[name].pop())

    def drain():
        for waits in flight.values():
            for ref, sem in waits:
                settle(ref, sem)

    barrier = pltpu.get_barrier_semaphore()

    @pl.loop(1, NR)
    def _(j):
        pl.semaphore_signal(barrier, inc=1, device_id={"row": row_peer(j)}, device_id_type=MESH)

    @pl.loop(1, NC)
    def _(j):
        pl.semaphore_signal(barrier, inc=1, device_id={"col": col_peer(j)}, device_id_type=MESH)

    across = lax.div(r, 2)
    for h in range(2):

        @pl.when(2 * c + h != r)
        def _():
            pl.semaphore_signal(
                barrier, inc=1, device_id={"row": 2 * c + h, "col": across}, device_id_type=MESH
            )

    block = 32

    @pl.loop(0, 256 // block)
    def _(b):
        ids = lax.broadcasted_iota(jnp.int32, (block, 256), 0) + b * block
        total = jnp.zeros((block, 256), F32)
        for n in range(32):
            total += jnp.where(ids == nbr_ref[n : n + 1, :], sw_ref[n : n + 1, :], 0.0)
        select[pl.ds(b * block, block), :] = total

    kinds = lax.broadcasted_iota(jnp.int32, (4, 256), 0)
    onehot = (kinds == types_ref[...]).astype(F32)
    mixed = env_ref[...] + dot3(te_ref[...], onehot, COLS)
    descriptor = dot3(mixed, select[...], NORMAL) / math.sqrt(32)
    hidden = jnp.tanh(descriptor)
    activity = jnp.tanh(dot3(hidden, w_ref[...], COLS))
    weighted = dot3(fw_ref[...], activity, NORMAL)
    scale = 1.0 / math.sqrt(256)
    predicted = jnp.sum(weighted * ow_ref[...], axis=1, keepdims=True) * scale
    error = tgt_ref[...] - predicted
    slopes = ow_ref[...] * (1.0 - activity * activity)
    jac = dot3(hidden * fw_ref[...], slopes, NORMAL) * scale

    for n in range(NC):
        jcol_send[n] = jac[4 * n : 4 * n + 4, :]
    for n in range(NR):
        jrow_send[n] = jac[2 * n : 2 * n + 2, :]
    e_send[0] = jnp.broadcast_to(error, (1, 128))
    cov_hi[...], cov_lo[...] = split(cov_ref[...])
    at = lax.broadcasted_iota(jnp.int32, (512, 512), 0)
    to = lax.broadcasted_iota(jnp.int32, (512, 512), 1)
    order[...] = (to == lax.rem(at, NC) * NR + lax.div(at, NC)).astype(F32).astype(BF16)

    mirror = lax.div(r, 2) == c
    pl.semaphore_wait(barrier, NR - 1 + NC - 1 + 2 - mirror.astype(jnp.int32))

    @pl.loop(1, NC)
    def _(j):
        p = col_peer(j)
        push("jcol", jcol_send.at[p], jc_recv.at[c], col=p)

    @pl.loop(1, NR)
    def _(j):
        p = row_peer(j)
        push("jrow", jrow_send.at[p], jr_recv.at[r], row=p)

    @pl.loop(1, NC)
    def _(j):
        push("err", e_send.at[0], e_recv.at[c], col=col_peer(j))

    track("jcol", jcol_send.at[pl.ds(0, NC - 1)], jc_recv.at[pl.ds(0, NC - 1)])
    track("jrow", jrow_send.at[pl.ds(0, NR - 1)], jr_recv.at[pl.ds(0, NR - 1)])
    track("err", e_recv.at[pl.ds(0, NC - 1)], e_recv.at[pl.ds(0, NC - 1)])
    jc_recv[c] = jcol_send[c]
    jr_recv[r] = jrow_send[r]
    e_recv[c] = e_send[0]

    land("jcol")
    jc_all[r] = jnp.concatenate([jc_recv[:, n, :] for n in range(4)], axis=1)

    for j in NEAR:
        push("jc_y", jc_all.at[r], jc_all.at[r], jc_y.at[j], row=y_peer(j))
    for i in (1, 3, 2):
        push("jc_x", jc_all.at[r], jc_all.at[r], jc_x.at[0], row=x_peer(i))
    track("jc_y", jc_all.at[pl.ds(0, NY - 1)])
    track("jc_x", jc_all.at[pl.ds(0, NR - NY)])

    land("jrow")
    jr_all[z, k] = jnp.concatenate([jr_recv[:, n, :] for n in range(2)], axis=1)
    for j in NEAR:
        push("jr_z", jr_all.at[z, k], jr_all.at[z, k], col=z_peer(j))
    track("jr_z", jr_all.at[pl.ds(0, NZ - 1), 0], jr_all.at[pl.ds(0, NZ - 1), 0])

    def pass_jc(j):
        slot = y_peer(NY - j)
        settle(jc_all.at[slot], jc_y.at[j])
        for i in (1, 3, 2):
            push("jc_x", jc_all.at[slot], jc_all.at[slot], jc_x.at[j], row=x_peer(i))

    cov = (cov_hi[...], cov_lo[...])
    for j in NEAR[:3]:
        pass_jc(j)
    for n, j in enumerate((0,) + NEAR):
        there = lax.rem(y + NY - j, NY)
        settle(jc_all.at[pl.ds(0, NX - 1)], jc_x.at[j])
        part = dot3(jc_all[pl.ds(there * NX, NX)].reshape(64, 512), cov, ROWS)
        w_send[there] = part.reshape(2, NR, 256)
        for h in range(2):

            @pl.when(2 * there + h != c)
            def _():
                push("w", w_send.at[there, h], w_recv.at[c], col=2 * there + h)

            @pl.when(2 * there + h == c)
            def _():
                w_recv[c] = w_send[there, h]

        if n + 3 < len(NEAR):
            pass_jc(NEAR[n + 3])
        if n == 5:
            land("jr_z")
            push("jr_p", jr_all.at[:, k], jr_all.at[:, k], col=partner)
            track("jr_p", jr_all.at[:, 0], jr_all.at[:, 0])
    track("w", w_recv.at[pl.ds(0, NC - 1)], w_recv.at[pl.ds(0, NC - 1)])

    land("err")
    lanes = lax.broadcasted_iota(jnp.int32, (NC, 128), 1)
    spots = lax.broadcasted_iota(jnp.int32, (NC, 128), 0)
    e_all[r] = jnp.sum(jnp.where(lanes == spots, e_recv[:, 0, :], 0.0), axis=0, keepdims=True)

    land("jr_p")
    jh, jl = split(jr_all[...].reshape(512, 256))
    perm = order[...]
    jr = (mm(perm, jh, NORMAL).astype(BF16), mm(perm, jl, NORMAL).astype(BF16))

    land("w")
    own = jnp.sum(w_recv[...], axis=0)
    art[z, k] = own

    for h in range(2):

        @pl.when(2 * c + h != r)
        def _():
            pltpu.make_async_remote_copy(
                src_ref=art.at[z, k, pl.ds(16 * h, 16)], dst_ref=turned.at[lax.rem(r, 2)],
                send_sem=turn_send.at[h], recv_sem=turn_recv.at[lax.rem(r, 2)],
                device_id={"row": 2 * c + h, "col": across}, device_id_type=MESH,
            ).start()

        @pl.when(2 * c + h == r)
        def _():
            turned[h] = own[16 * h : 16 * h + 16, :]

    s_part = dot3(own, jr, ROWS)
    for n in range(NX):
        s_send[n] = s_part[8 * n : 8 * n + 8, :]
    for i in (1, 3, 2):
        push("s_x", s_send.at[lax.rem(x + i, NX)], s_x.at[x], row=x_peer(i))
    track("s_x", s_x.at[pl.ds(0, NX - 1)], s_x.at[pl.ds(0, NX - 1)])
    s_x[x] = s_send[x]

    for j in NEAR:
        push("art_z", art.at[z, k], art.at[z, k], col=z_peer(j))
    track("art_z", art.at[pl.ds(0, NZ - 1), 0], art.at[pl.ds(0, NZ - 1), 0])

    land("s_x")
    s_y[y] = jnp.sum(s_x[...], axis=0)
    for j in NEAR:
        push("s_y", s_y.at[y], s_y.at[y], row=y_peer(j))
    track("s_y", s_y.at[pl.ds(0, NY - 1)], s_y.at[pl.ds(0, NY - 1)])

    for h in range(2):

        @pl.when(2 * c + h != r)
        def _():
            settle(turned.at[h], turn_recv.at[h])
            settle(turned.at[h], turn_send.at[h])

    act[r] = jnp.concatenate([turned[0], turned[1]], axis=1)
    for j in NEAR:
        push("act_y", act.at[r], act.at[r], act_y.at[j], row=y_peer(j))
    for i in (1, 3, 2):
        push("act_x", act.at[r], act.at[r], row=x_peer(i))
    track("act_y", act.at[pl.ds(0, NY - 1)])

    land("s_y")
    mine = c * NX + x
    s_all[mine] = jnp.sum(s_y[...], axis=0)
    for j in NEAR:
        push("s_z", s_all.at[mine], s_all.at[mine], s_z.at[j], col=z_peer(j))
    for i in (1, 3, 2):
        push("s_g", s_all.at[mine], s_all.at[mine], s_g.at[0], row=x_peer(i))
    track("s_z", s_all.at[pl.ds(0, NZ - 1)])

    land("art_z")
    push("art_p", art.at[:, k], art.at[:, k], col=partner)
    track("art_p", art.at[:, 0], art.at[:, 0])

    @pl.loop(1, NR)
    def _(j):
        push("e", e_all.at[r], e_all.at[r], row=row_peer(j))

    track("e", e_all.at[pl.ds(0, NR - 1)], e_all.at[pl.ds(0, NR - 1)])

    for j in NEAR:
        slot = z_peer(NZ - j) * NX + x
        settle(s_all.at[slot], s_z.at[j])
        for i in (1, 3, 2):
            push("s_g", s_all.at[slot], s_all.at[slot], s_g.at[j], row=x_peer(i))
        slot = y_peer(NY - j)
        settle(act.at[slot], act_y.at[j])
        for i in (1, 3, 2):
            push("act_x", act.at[slot], act.at[slot], row=x_peer(i))
    track("s_g", s_all.at[pl.ds(0, NX * NZ - NZ)])
    track("act_x", act.at[pl.ds(0, NR - NY)], act.at[pl.ds(0, NR - NY)])
    for j in (0,) + NEAR:
        settle(s_all.at[pl.ds(0, NX - 1)], s_g.at[j])
        group = pl.ds(z_peer(NZ - j) * NX, NX)
        push("s_p", s_all.at[group], s_all.at[group], col=partner)
    track("s_p", s_all.at[pl.ds(0, NX * NZ)], s_all.at[pl.ds(0, NX * NZ)])
    land("s_p")

    eye = at == to
    innovation = s_all[...].reshape(512, 512) + jnp.where(eye, FORGET, 0.0)
    bound = jnp.max(jnp.sum(jnp.abs(innovation), axis=0, keepdims=True), axis=1, keepdims=True)
    land("art_p")
    power = split(jnp.where(eye, 1.0, 0.0) - innovation / bound)
    gain = art[...].reshape(512, 256) / bound
    for step in range(4):
        gain = gain + dot3(power, gain, NORMAL)
        if step < 3:
            power = split(dot3(power, power, NORMAL))

    land("e")
    spread = (
        lax.broadcasted_iota(jnp.int32, (512, NR), 1)
        == lax.div(lax.broadcasted_iota(jnp.int32, (512, NR), 0), NC)
    ).astype(F32)
    errors = jnp.concatenate([e_all[n] for n in range(NR)], axis=0)
    picked = jnp.dot(spread, errors, precision=lax.Precision.HIGHEST)
    own_lane = lax.broadcasted_iota(jnp.int32, (512, 128), 1) == lax.rem(
        lax.broadcasted_iota(jnp.int32, (512, 128), 0), NC
    )
    column = jnp.sum(jnp.where(own_lane, picked, 0.0), axis=1, keepdims=True)
    delta = jnp.sum(gain * column, axis=0, keepdims=True)
    half = lax.div(c, 8)
    delta = jnp.where(half == 0, delta[:, :128], delta[:, 128:])
    moved = w_ref[pl.ds(2 * r + half, 1), :] + delta
    moved = pltpu.roll(moved, 128 - 16 * lax.rem(c, 8), 1)
    weight_ref[...] = moved[:, :16]

    land("act_x")
    update = dot3(gain, act[...].reshape(512, 512), COLS)
    newcov_ref[...] = (cov_ref[...] - update) * (1.0 / FORGET)
    drain()


def on_device(
    atom_types, neighbor_ids, switching, environment, force_weights, targets,
    type_embed, layer_weight, out_weight, covariance,
):
    vmem = pl.BlockSpec(memory_space=pltpu.VMEM)
    V = pltpu.VMEM
    D = pltpu.SemaphoreType.DMA
    scratch = [
        V((256, 256), F32), V((256, 512), BF16), V((256, 512), BF16), V((512, 512), BF16),
        V((NR, 2, 128), F32), V((NC, 4, 128), F32), V((1, 1, 128), F32),
        V((NR, 2, 128), F32), V((NC, 4, 128), F32), V((NC, 1, 128), F32), V((NR, 1, 128), F32),
        V((NZ, 2, NR, 256), F32), V((NR, NC, 512), F32),
        V((NY, 2, NR, 256), F32), V((NC, NR, 256), F32), V((NZ, 2, NR, 256), F32),
        V((2, 16, 256), F32), V((NR, 16, 512), F32),
        V((NX, 8, 512), F32), V((NX, 8, 512), F32), V((NY, 8, 512), F32), V((NC * NX, 8, 512), F32),
        D((len(GROUPS),)), D((len(GROUPS),)), D((NY,)), D((NY,)), D((NY,)), D((NZ,)), D((NZ,)),
        D((2,)), D((2,)),
    ]
    new_cov, weight = pl.pallas_call(
        kernel,
        out_shape=(
            jax.ShapeDtypeStruct((256, 512), F32),
            jax.ShapeDtypeStruct((1, 16), F32),
        ),
        in_specs=[vmem] * 10,
        out_specs=(vmem, vmem),
        scratch_shapes=scratch,
        compiler_params=pltpu.CompilerParams(
            collective_id=0, has_side_effects=True, vmem_limit_bytes=60 * 1024 * 1024
        ),
    )(
        atom_types, neighbor_ids[0], switching[0], environment[0].T, force_weights,
        targets.reshape(1, 1), type_embed, layer_weight, out_weight.reshape(1, 128), covariance,
    )
    return (weight.reshape(16), new_cov)


def solution(mesh):
    in_specs = (
        P(("row", "col"), None),
        P(("row", "col"), None, None),
        P(("row", "col"), None, None),
        P(("row", "col"), None, None),
        P(("row", "col"), None),
        P(("row", "col")),
        P(),
        P(),
        P(),
        P("row", "col"),
    )
    out_specs = (P(("row", "col")), P("row", "col"))
    return jax.shard_map(
        on_device, mesh=mesh, in_specs=in_specs, out_specs=out_specs, check_vma=False
    )
```

```python
import functools
import math

import jax
import jax.numpy as jnp
from jax import lax
from jax.experimental import pallas as pl
from jax.experimental.pallas import tpu as pltpu
from jax.sharding import PartitionSpec as P

FORGET = 0.98
MESH = pl.DeviceIdType.MESH
F32 = jnp.float32
BF16 = jnp.bfloat16
NX, NY, NZ = 4, 8, 8
NR, NC = 32, 16
NEAR = (1, 7, 2, 6, 3, 5, 4)
GROUPS = (
    "jcol", "jrow", "err", "jc_y", "jc_x", "jr_z", "jr_p", "e", "w", "art_z", "art_p",
    "s", "s_yz", "s_x", "s_p", "act", "act_x",
)


def split(a):
    hi = a.astype(BF16)
    lo = (a - hi.astype(F32)).astype(BF16)
    return hi, lo


def mm(a, b, dims):
    return lax.dot_general(a, b, (dims, ((), ())), preferred_element_type=F32)


def dot3(a, b, dims):
    ah, al = a if isinstance(a, tuple) else split(a)
    bh, bl = b if isinstance(b, tuple) else split(b)
    return mm(ah, bh, dims) + (mm(ah, bl, dims) + mm(al, bh, dims))


ROWS = ((1,), (1,))
COLS = ((0,), (0,))
NORMAL = ((1,), (0,))


def kernel(
    types_ref, nbr_ref, sw_ref, env_ref, fw_ref, tgt_ref, te_ref, w_ref, ow_ref, cov_ref,
    newcov_ref, weight_ref,
    select, cov_hi, cov_lo, order, jrow_send, jcol_send, e_send, jr_recv, jc_recv, e_recv, e_all,
    jr_all, jc_all, w_send, w_recv, art, act,
    s_send, s_recv, s_rows, s_all,
    send, recv, jc_y, jc_x, act_in, act_x,
):
    r = lax.axis_index("row")
    c = lax.axis_index("col")
    x, y = lax.rem(r, NX), lax.div(r, NX)
    k, z = lax.rem(c, 2), lax.div(c, 2)

    def row_peer(j):
        return lax.rem(r + j, NR)

    def col_peer(j):
        return lax.rem(c + j, NC)

    def x_peer(j):
        return y * NX + lax.rem(x + j, NX)

    def y_peer(j):
        return lax.rem(y + j, NY) * NX + x

    def z_peer(j):
        return lax.rem(z + j, NZ) * 2 + k

    partner = z * 2 + 1 - k
    flight = {}

    def push(name, src, dst, sem=None, **where):
        at = GROUPS.index(name)
        pltpu.make_async_remote_copy(
            src_ref=src, dst_ref=dst, send_sem=send.at[at],
            recv_sem=recv.at[at] if sem is None else sem,
            device_id=where, device_id_type=MESH,
        ).start()

    def settle(ref, sem):
        pltpu.make_async_copy(ref, ref, sem).wait()

    def track(name, sent, got=None):
        at = GROUPS.index(name)
        flight[name] = [(sent, send.at[at])]
        if got is not None:
            flight[name].append((got, recv.at[at]))

    def land(name):
        settle(*flight[name].pop())

    def drain():
        for waits in flight.values():
            for ref, sem in waits:
                settle(ref, sem)

    barrier = pltpu.get_barrier_semaphore()

    @pl.loop(1, NR)
    def _(j):
        pl.semaphore_signal(barrier, inc=1, device_id={"row": row_peer(j)}, device_id_type=MESH)

    @pl.loop(1, NC)
    def _(j):
        pl.semaphore_signal(barrier, inc=1, device_id={"col": col_peer(j)}, device_id_type=MESH)

    across = lax.div(r, 2)
    source = z * NX + x
    takes = lax.div(x, 2) == k
    half = lax.rem(x, 2)

    @pl.when(takes)
    def _():
        @pl.loop(0, NC)
        def _(p):
            @pl.when((source != r) | (p != c))
            def _():
                pl.semaphore_signal(
                    barrier, inc=1, device_id={"row": source, "col": p}, device_id_type=MESH
                )

    own_target = across == c

    block = 32

    @pl.loop(0, 256 // block)
    def _(b):
        ids = lax.broadcasted_iota(jnp.int32, (block, 256), 0) + b * block
        total = jnp.zeros((block, 256), F32)
        for n in range(32):
            total += jnp.where(ids == nbr_ref[n : n + 1, :], sw_ref[n : n + 1, :], 0.0)
        select[pl.ds(b * block, block), :] = total

    kinds = lax.broadcasted_iota(jnp.int32, (4, 256), 0)
    onehot = (kinds == types_ref[...]).astype(F32)
    mixed = env_ref[...] + dot3(te_ref[...], onehot, COLS)
    descriptor = dot3(mixed, select[...], NORMAL) / math.sqrt(32)
    hidden = jnp.tanh(descriptor)
    activity = jnp.tanh(dot3(hidden, w_ref[...], COLS))
    weighted = dot3(fw_ref[...], activity, NORMAL)
    scale = 1.0 / math.sqrt(256)
    predicted = jnp.sum(weighted * ow_ref[...], axis=1, keepdims=True) * scale
    error = tgt_ref[...] - predicted
    slopes = ow_ref[...] * (1.0 - activity * activity)
    jac = dot3(hidden * fw_ref[...], slopes, NORMAL) * scale

    for n in range(NC):
        jcol_send[n] = jac[4 * n : 4 * n + 4, :]
    for n in range(NR):
        jrow_send[n] = jac[2 * n : 2 * n + 2, :]
    e_send[0] = jnp.broadcast_to(error, (1, 128))
    cov_hi[...], cov_lo[...] = split(cov_ref[...])
    at = lax.broadcasted_iota(jnp.int32, (512, 512), 0)
    to = lax.broadcasted_iota(jnp.int32, (512, 512), 1)
    order[...] = (to == lax.rem(at, NC) * NR + lax.div(at, NC)).astype(F32).astype(BF16)

    pl.semaphore_wait(barrier, NR - 1 + NC - 1 + NY - own_target.astype(jnp.int32))

    @pl.loop(1, NC)
    def _(j):
        p = col_peer(j)
        push("jcol", jcol_send.at[p], jc_recv.at[c], col=p)

    @pl.loop(1, NR)
    def _(j):
        p = row_peer(j)
        push("jrow", jrow_send.at[p], jr_recv.at[r], row=p)

    @pl.loop(1, NC)
    def _(j):
        push("err", e_send.at[0], e_recv.at[c], col=col_peer(j))

    track("jcol", jcol_send.at[pl.ds(0, NC - 1)], jc_recv.at[pl.ds(0, NC - 1)])
    track("jrow", jrow_send.at[pl.ds(0, NR - 1)], jr_recv.at[pl.ds(0, NR - 1)])
    track("err", e_recv.at[pl.ds(0, NC - 1)], e_recv.at[pl.ds(0, NC - 1)])
    jc_recv[c] = jcol_send[c]
    jr_recv[r] = jrow_send[r]
    e_recv[c] = e_send[0]

    land("jcol")
    jc_all[r] = jnp.concatenate([jc_recv[:, n, :] for n in range(4)], axis=1)

    for j in NEAR:
        push("jc_y", jc_all.at[r], jc_all.at[r], jc_y.at[j], row=y_peer(j))
    for i in (1, 3, 2):
        push("jc_x", jc_all.at[r], jc_all.at[r], jc_x.at[0], row=x_peer(i))
    track("jc_y", jc_all.at[pl.ds(0, NY - 1)])
    track("jc_x", jc_all.at[pl.ds(0, NR - NY)])

    land("jrow")
    jr_all[z, k] = jnp.concatenate([jr_recv[:, n, :] for n in range(2)], axis=1)
    for j in NEAR:
        push("jr_z", jr_all.at[z, k], jr_all.at[z, k], col=z_peer(j))
    track("jr_z", jr_all.at[pl.ds(0, NZ - 1), 0], jr_all.at[pl.ds(0, NZ - 1), 0])

    def pass_jc(j):
        slot = y_peer(NY - j)
        settle(jc_all.at[slot], jc_y.at[j])
        for i in (1, 3, 2):
            push("jc_x", jc_all.at[slot], jc_all.at[slot], jc_x.at[j], row=x_peer(i))

    cov = (cov_hi[...], cov_lo[...])
    for j in NEAR[:3]:
        pass_jc(j)
    for n, j in enumerate((0,) + NEAR):
        there = lax.rem(y + NY - j, NY)
        settle(jc_all.at[pl.ds(0, NX - 1)], jc_x.at[j])
        part = dot3(jc_all[pl.ds(there * NX, NX)].reshape(64, 512), cov, ROWS)
        w_send[there] = part.reshape(2, NR, 256)
        for h in range(2):

            @pl.when(2 * there + h != c)
            def _():
                push("w", w_send.at[there, h], w_recv.at[c], col=2 * there + h)

            @pl.when(2 * there + h == c)
            def _():
                w_recv[c] = w_send[there, h]

        if n + 3 < len(NEAR):
            pass_jc(NEAR[n + 3])
        if n == 5:
            land("jr_z")
            push("jr_p", jr_all.at[:, k], jr_all.at[:, k], col=partner)
            track("jr_p", jr_all.at[:, 0], jr_all.at[:, 0])
    track("w", w_recv.at[pl.ds(0, NC - 1)], w_recv.at[pl.ds(0, NC - 1)])

    land("err")
    lanes = lax.broadcasted_iota(jnp.int32, (NC, 128), 1)
    spots = lax.broadcasted_iota(jnp.int32, (NC, 128), 0)
    e_all[r] = jnp.sum(jnp.where(lanes == spots, e_recv[:, 0, :], 0.0), axis=0, keepdims=True)

    land("jr_p")
    jh, jl = split(jr_all[...].reshape(512, 256))
    perm = order[...]
    jr = (mm(perm, jh, NORMAL).astype(BF16), mm(perm, jl, NORMAL).astype(BF16))

    land("w")
    own = jnp.sum(w_recv[...], axis=0)
    art[z, k] = own

    for j in (0,) + NEAR:
        to_row = y_peer(j)
        if j == 0:

            @pl.when(jnp.logical_not(own_target))
            def _():
                push("act", art.at[z, k], act.at[half, c], act_in.at[c], row=to_row, col=across)

            @pl.when(own_target)
            def _():
                act[half, c] = own

        else:
            push("act", art.at[z, k], act.at[half, c], act_in.at[c], row=to_row, col=across)
    track("act", art.at[pl.ds(0, NY - 1), 0])

    s_part = dot3(own, jr, ROWS)
    for n in range(4):
        s_send[:, n, :] = s_part[:, 128 * n : 128 * n + 128]

    @pl.loop(1, NR)
    def _(j):
        p = row_peer(j)
        push("s", s_send.at[lax.rem(p, NX) * NY + lax.div(p, NX)], s_recv.at[r], row=p)

    track("s", s_send.at[pl.ds(0, NR - 1)], s_recv.at[pl.ds(0, NR - 1)])
    s_recv[r] = s_send[x * NY + y]

    for j in NEAR:
        push("art_z", art.at[z, k], art.at[z, k], col=z_peer(j))
    track("art_z", art.at[pl.ds(0, NZ - 1), 0], art.at[pl.ds(0, NZ - 1), 0])

    land("s")
    spot = z * NY + y
    s_rows[spot] = jnp.sum(s_recv[...], axis=0)

    @pl.loop(1, NY * NZ)
    def _(j):
        to_row = lax.rem(y + lax.div(j, NZ), NY) * NX + x
        to_col = lax.rem(z + lax.rem(j, NZ), NZ) * 2 + k
        push("s_yz", s_rows.at[spot], s_rows.at[spot], row=to_row, col=to_col)

    most = s_rows.at[pl.ds(0, NY * NZ - 1)]
    track("s_yz", most, most)

    @pl.when(takes)
    def _():
        for j in (0, 1, 7, 2, 6, 3, 5, 4):
            for h in range(2):
                p = lax.rem(z + j, NZ) * 2 + h

                @pl.when((source != r) | (p != c))
                def _():
                    settle(act.at[half, p], act_in.at[p])

                for i in (1, 3, 2):
                    push("act_x", act.at[half, p], act.at[half, p], act_x.at[half], row=x_peer(i))

    land("art_z")
    push("art_p", art.at[:, k], art.at[:, k], col=partner)
    track("art_p", art.at[:, 0], art.at[:, 0])

    @pl.loop(1, NR)
    def _(j):
        push("e", e_all.at[r], e_all.at[r], row=row_peer(j))

    track("e", e_all.at[pl.ds(0, NR - 1)], e_all.at[pl.ds(0, NR - 1)])

    land("s_yz")
    for n in range(NZ):
        s_all[n, k, x] = jnp.concatenate([s_rows[NY * n : NY * n + NY, i, :] for i in range(4)], axis=1)
    for i in (1, 3, 2):
        push("s_x", s_all.at[:, k, x], s_all.at[:, k, x], row=x_peer(i))
    track("s_x", s_all.at[:, 0, pl.ds(0, NX - 1)], s_all.at[:, 0, pl.ds(0, NX - 1)])
    land("s_x")
    push("s_p", s_all.at[:, k], s_all.at[:, k], col=partner)
    track("s_p", s_all.at[:, 0], s_all.at[:, 0])
    land("s_p")

    eye = at == to
    innovation = s_all[...].reshape(512, 512) + jnp.where(eye, FORGET, 0.0)
    bound = jnp.max(jnp.sum(jnp.abs(innovation), axis=0, keepdims=True), axis=1, keepdims=True)
    land("art_p")
    power = split(jnp.where(eye, 1.0, 0.0) - innovation / bound)
    gain = art[...].reshape(512, 256) / bound
    for step in range(4):
        gain = gain + dot3(power, gain, NORMAL)
        if step < 3:
            power = split(dot3(power, power, NORMAL))

    land("e")
    spread = (
        lax.broadcasted_iota(jnp.int32, (512, NR), 1)
        == lax.div(lax.broadcasted_iota(jnp.int32, (512, NR), 0), NC)
    ).astype(F32)
    errors = jnp.concatenate([e_all[n] for n in range(NR)], axis=0)
    picked = jnp.dot(spread, errors, precision=lax.Precision.HIGHEST)
    own_lane = lax.broadcasted_iota(jnp.int32, (512, 128), 1) == lax.rem(
        lax.broadcasted_iota(jnp.int32, (512, 128), 0), NC
    )
    column = jnp.sum(jnp.where(own_lane, picked, 0.0), axis=1, keepdims=True)
    delta = jnp.sum(gain * column, axis=0, keepdims=True)
    upper = lax.div(c, 8)
    delta = jnp.where(upper == 0, delta[:, :128], delta[:, 128:])
    moved = w_ref[pl.ds(2 * r + upper, 1), :] + delta
    moved = pltpu.roll(moved, 128 - 16 * lax.rem(c, 8), 1)
    weight_ref[...] = moved[:, :16]

    for h in range(2):

        @pl.when(jnp.logical_not(takes & (half == h)))
        def _():
            settle(act.at[h], act_x.at[h])

    gain = split(gain)
    for h in range(2):
        update = dot3(gain, act[h].reshape(512, 256), COLS)
        columns = slice(256 * h, 256 * h + 256)
        newcov_ref[:, columns] = (cov_ref[:, columns] - update) * (1.0 / FORGET)

    @pl.when(jnp.logical_not(own_target))
    def _():
        settle(art.at[0, 0], send.at[GROUPS.index("act")])

    @pl.when(takes)
    def _():
        for i in range(3):
            settle(act.at[0], send.at[GROUPS.index("act_x")])

    drain()


def on_device(
    atom_types, neighbor_ids, switching, environment, force_weights, targets,
    type_embed, layer_weight, out_weight, covariance,
):
    vmem = pl.BlockSpec(memory_space=pltpu.VMEM)
    V = pltpu.VMEM
    D = pltpu.SemaphoreType.DMA
    scratch = [
        V((256, 256), F32), V((256, 512), BF16), V((256, 512), BF16), V((512, 512), BF16),
        V((NR, 2, 128), F32), V((NC, 4, 128), F32), V((1, 1, 128), F32),
        V((NR, 2, 128), F32), V((NC, 4, 128), F32), V((NC, 1, 128), F32), V((NR, 1, 128), F32),
        V((NZ, 2, NR, 256), F32), V((NR, NC, 512), F32),
        V((NY, 2, NR, 256), F32), V((NC, NR, 256), F32), V((NZ, 2, NR, 256), F32),
        V((2, NC, NR, 256), F32),
        V((NR, 4, 128), F32), V((NR, 4, 128), F32), V((NZ * NY, 4, 128), F32), V((NZ, 2, NX, 8, 512), F32),
        D((len(GROUPS),)), D((len(GROUPS),)), D((NY,)), D((NY,)), D((NC,)), D((2,)),
    ]
    new_cov, weight = pl.pallas_call(
        kernel,
        out_shape=(
            jax.ShapeDtypeStruct((256, 512), F32),
            jax.ShapeDtypeStruct((1, 16), F32),
        ),
        in_specs=[vmem] * 10,
        out_specs=(vmem, vmem),
        scratch_shapes=scratch,
        compiler_params=pltpu.CompilerParams(
            collective_id=0, has_side_effects=True, vmem_limit_bytes=60 * 1024 * 1024
        ),
    )(
        atom_types, neighbor_ids[0], switching[0], environment[0].T, force_weights,
        targets.reshape(1, 1), type_embed, layer_weight, out_weight.reshape(1, 128), covariance,
    )
    return (weight.reshape(16), new_cov)


def solution(mesh):
    in_specs = (
        P(("row", "col"), None),
        P(("row", "col"), None, None),
        P(("row", "col"), None, None),
        P(("row", "col"), None, None),
        P(("row", "col"), None),
        P(("row", "col")),
        P(),
        P(),
        P(),
        P("row", "col"),
    )
    out_specs = (P(("row", "col")), P("row", "col"))
    return jax.shard_map(
        on_device, mesh=mesh, in_specs=in_specs, out_specs=out_specs, check_vma=False
    )
```

```python
import functools
import math

import jax
import jax.numpy as jnp
from jax import lax
from jax.experimental import pallas as pl
from jax.experimental.pallas import tpu as pltpu
from jax.sharding import PartitionSpec as P

FORGET = 0.98
MESH = pl.DeviceIdType.MESH
F32 = jnp.float32
BF16 = jnp.bfloat16
NX, NY, NZ = 4, 8, 8
NR, NC = 32, 16
NEAR = (1, 7, 2, 6, 3, 5, 4)
GROUPS = (
    "jcol", "jrow", "err", "jc_y", "jc_x", "jr_z", "jr_p", "e", "w", "art_z", "art_p",
    "s", "s_yz", "s_x", "s_p", "act", "act_x",
)


def split(a):
    hi = a.astype(BF16)
    lo = (a - hi.astype(F32)).astype(BF16)
    return hi, lo


def mm(a, b, dims):
    return lax.dot_general(a, b, (dims, ((), ())), preferred_element_type=F32)


def dot3(a, b, dims):
    ah, al = a if isinstance(a, tuple) else split(a)
    bh, bl = b if isinstance(b, tuple) else split(b)
    return mm(ah, bh, dims) + (mm(ah, bl, dims) + mm(al, bh, dims))


ROWS = ((1,), (1,))
COLS = ((0,), (0,))
NORMAL = ((1,), (0,))


def kernel(
    types_ref, nbr_ref, sw_ref, env_ref, fw_ref, tgt_ref, te_ref, w_ref, ow_ref, cov_ref,
    gain_ref, act, weight_ref,
    select, cov_hi, cov_lo, order, jrow_send, jcol_send, e_send, jr_recv, jc_recv, e_recv, e_all,
    jr_all, jc_all, w_send, w_recv, art,
    s_send, s_recv, s_rows, s_all,
    send, recv, jc_y, jc_x, act_in, act_x, s_g,
):
    r = lax.axis_index("row")
    c = lax.axis_index("col")
    x, y = lax.rem(r, NX), lax.div(r, NX)
    k, z = lax.rem(c, 2), lax.div(c, 2)

    def row_peer(j):
        return lax.rem(r + j, NR)

    def col_peer(j):
        return lax.rem(c + j, NC)

    def x_peer(j):
        return y * NX + lax.rem(x + j, NX)

    def y_peer(j):
        return lax.rem(y + j, NY) * NX + x

    def z_peer(j):
        return lax.rem(z + j, NZ) * 2 + k

    partner = z * 2 + 1 - k
    flight = {}

    def push(name, src, dst, sem=None, **where):
        at = GROUPS.index(name)
        pltpu.make_async_remote_copy(
            src_ref=src, dst_ref=dst, send_sem=send.at[at],
            recv_sem=recv.at[at] if sem is None else sem,
            device_id=where, device_id_type=MESH,
        ).start()

    def settle(ref, sem):
        pltpu.make_async_copy(ref, ref, sem).wait()

    def track(name, sent, got=None):
        at = GROUPS.index(name)
        flight[name] = [(sent, send.at[at])]
        if got is not None:
            flight[name].append((got, recv.at[at]))

    def land(name):
        settle(*flight[name].pop())

    def drain():
        for waits in flight.values():
            for ref, sem in waits:
                settle(ref, sem)

    barrier = pltpu.get_barrier_semaphore()

    @pl.loop(1, NR)
    def _(j):
        pl.semaphore_signal(barrier, inc=1, device_id={"row": row_peer(j)}, device_id_type=MESH)

    @pl.loop(1, NC)
    def _(j):
        pl.semaphore_signal(barrier, inc=1, device_id={"col": col_peer(j)}, device_id_type=MESH)

    across = lax.div(r, 2)
    source = z * NX + x
    takes = lax.div(x, 2) == k
    half = lax.rem(x, 2)

    @pl.when(takes)
    def _():
        @pl.loop(0, NC)
        def _(p):
            @pl.when((source != r) | (p != c))
            def _():
                pl.semaphore_signal(
                    barrier, inc=1, device_id={"row": source, "col": p}, device_id_type=MESH
                )

    own_target = across == c

    block = 32

    @pl.loop(0, 256 // block)
    def _(b):
        ids = lax.broadcasted_iota(jnp.int32, (block, 256), 0) + b * block
        total = jnp.zeros((block, 256), F32)
        for n in range(32):
            total += jnp.where(ids == nbr_ref[n : n + 1, :], sw_ref[n : n + 1, :], 0.0)
        select[pl.ds(b * block, block), :] = total

    kinds = lax.broadcasted_iota(jnp.int32, (4, 256), 0)
    onehot = (kinds == types_ref[...]).astype(F32)
    mixed = env_ref[...] + dot3(te_ref[...], onehot, COLS)
    descriptor = dot3(mixed, select[...], NORMAL) / math.sqrt(32)
    hidden = jnp.tanh(descriptor)
    activity = jnp.tanh(dot3(hidden, w_ref[...], COLS))
    weighted = dot3(fw_ref[...], activity, NORMAL)
    scale = 1.0 / math.sqrt(256)
    predicted = jnp.sum(weighted * ow_ref[...], axis=1, keepdims=True) * scale
    error = tgt_ref[...] - predicted
    slopes = ow_ref[...] * (1.0 - activity * activity)
    jac = dot3(hidden * fw_ref[...], slopes, NORMAL) * scale

    for n in range(NC):
        jcol_send[n] = jac[4 * n : 4 * n + 4, :]
    for n in range(NR):
        jrow_send[n] = jac[2 * n : 2 * n + 2, :]
    e_send[0] = jnp.broadcast_to(error, (1, 128))
    cov_hi[...], cov_lo[...] = split(cov_ref[...])
    at = lax.broadcasted_iota(jnp.int32, (512, 512), 0)
    to = lax.broadcasted_iota(jnp.int32, (512, 512), 1)
    order[...] = (to == lax.rem(at, NC) * NR + lax.div(at, NC)).astype(F32).astype(BF16)

    pl.semaphore_wait(barrier, NR - 1 + NC - 1 + NY - own_target.astype(jnp.int32))

    @pl.loop(1, NC)
    def _(j):
        p = col_peer(j)
        push("jcol", jcol_send.at[p], jc_recv.at[c], col=p)

    @pl.loop(1, NR)
    def _(j):
        p = row_peer(j)
        push("jrow", jrow_send.at[p], jr_recv.at[r], row=p)

    @pl.loop(1, NC)
    def _(j):
        push("err", e_send.at[0], e_recv.at[c], col=col_peer(j))

    track("jcol", jcol_send.at[pl.ds(0, NC - 1)], jc_recv.at[pl.ds(0, NC - 1)])
    track("jrow", jrow_send.at[pl.ds(0, NR - 1)], jr_recv.at[pl.ds(0, NR - 1)])
    track("err", e_recv.at[pl.ds(0, NC - 1)], e_recv.at[pl.ds(0, NC - 1)])
    jc_recv[c] = jcol_send[c]
    jr_recv[r] = jrow_send[r]
    e_recv[c] = e_send[0]

    land("jcol")
    jc_all[r] = jnp.concatenate([jc_recv[:, n, :] for n in range(4)], axis=1)

    for j in NEAR:
        push("jc_y", jc_all.at[r], jc_all.at[r], jc_y.at[j], row=y_peer(j))
    for i in (1, 3, 2):
        push("jc_x", jc_all.at[r], jc_all.at[r], jc_x.at[0], row=x_peer(i))
    track("jc_y", jc_all.at[pl.ds(0, NY - 1)])
    track("jc_x", jc_all.at[pl.ds(0, NR - NY)])

    land("jrow")
    jr_all[z, k] = jnp.concatenate([jr_recv[:, n, :] for n in range(2)], axis=1)
    for j in NEAR:
        push("jr_z", jr_all.at[z, k], jr_all.at[z, k], col=z_peer(j))
    track("jr_z", jr_all.at[pl.ds(0, NZ - 1), 0], jr_all.at[pl.ds(0, NZ - 1), 0])

    def pass_jc(j):
        slot = y_peer(NY - j)
        settle(jc_all.at[slot], jc_y.at[j])
        for i in (1, 3, 2):
            push("jc_x", jc_all.at[slot], jc_all.at[slot], jc_x.at[j], row=x_peer(i))

    cov = (cov_hi[...], cov_lo[...])
    for j in NEAR[:3]:
        pass_jc(j)
    for n, j in enumerate((0,) + NEAR):
        there = lax.rem(y + NY - j, NY)
        settle(jc_all.at[pl.ds(0, NX - 1)], jc_x.at[j])
        part = dot3(jc_all[pl.ds(there * NX, NX)].reshape(64, 512), cov, ROWS)
        w_send[there] = part.reshape(2, NR, 256)
        for h in range(2):

            @pl.when(2 * there + h != c)
            def _():
                push("w", w_send.at[there, h], w_recv.at[c], col=2 * there + h)

            @pl.when(2 * there + h == c)
            def _():
                w_recv[c] = w_send[there, h]

        if n + 3 < len(NEAR):
            pass_jc(NEAR[n + 3])
        if n == 5:
            land("jr_z")
            push("jr_p", jr_all.at[:, k], jr_all.at[:, k], col=partner)
            track("jr_p", jr_all.at[:, 0], jr_all.at[:, 0])
    track("w", w_recv.at[pl.ds(0, NC - 1)], w_recv.at[pl.ds(0, NC - 1)])

    land("err")
    lanes = lax.broadcasted_iota(jnp.int32, (NC, 128), 1)
    spots = lax.broadcasted_iota(jnp.int32, (NC, 128), 0)
    e_all[r] = jnp.sum(jnp.where(lanes == spots, e_recv[:, 0, :], 0.0), axis=0, keepdims=True)

    land("jr_p")
    jh, jl = split(jr_all[...].reshape(512, 256))
    perm = order[...]
    jr = (mm(perm, jh, NORMAL).astype(BF16), mm(perm, jl, NORMAL).astype(BF16))

    land("w")
    own = jnp.sum(w_recv[...], axis=0)
    art[z, k] = own

    s_part = dot3(own, jr, ROWS)
    for n in range(4):
        s_send[:, n, :] = s_part[:, 128 * n : 128 * n + 128]

    @pl.loop(1, NR)
    def _(j):
        p = row_peer(j)
        push("s", s_send.at[lax.rem(p, NX) * NY + lax.div(p, NX)], s_recv.at[r], row=p)

    track("s", s_send.at[pl.ds(0, NR - 1)], s_recv.at[pl.ds(0, NR - 1)])
    s_recv[r] = s_send[x * NY + y]

    for j in (0,) + NEAR:
        to_row = y_peer(j)
        if j == 0:

            @pl.when(jnp.logical_not(own_target))
            def _():
                push("act", art.at[z, k], act.at[half, c], act_in.at[c], row=to_row, col=across)

            @pl.when(own_target)
            def _():
                act[half, c] = own

        else:
            push("act", art.at[z, k], act.at[half, c], act_in.at[c], row=to_row, col=across)
    track("act", art.at[pl.ds(0, NY - 1), 0])

    land("s")
    spot = z * NY + y
    s_rows[spot] = jnp.sum(s_recv[...], axis=0)

    @pl.loop(1, NY * NZ)
    def _(j):
        to_row = lax.rem(y + lax.div(j, NZ), NY) * NX + x
        to_col = lax.rem(z + lax.rem(j, NZ), NZ) * 2 + k
        push("s_yz", s_rows.at[spot], s_rows.at[spot], row=to_row, col=to_col)

    most = s_rows.at[pl.ds(0, NY * NZ - 1)]
    track("s_yz", most, most)

    for j in NEAR:
        push("art_z", art.at[z, k], art.at[z, k], col=z_peer(j))
    track("art_z", art.at[pl.ds(0, NZ - 1), 0], art.at[pl.ds(0, NZ - 1), 0])

    @pl.when(takes)
    def _():
        for j in (0, 1, 7, 2, 6, 3, 5, 4):
            for h in range(2):
                p = lax.rem(z + j, NZ) * 2 + h

                @pl.when((source != r) | (p != c))
                def _():
                    settle(act.at[half, p], act_in.at[p])

                for i in (1, 3, 2):
                    push("act_x", act.at[half, p], act.at[half, p], act_x.at[half], row=x_peer(i))

    @pl.loop(1, NR)
    def _(j):
        push("e", e_all.at[r], e_all.at[r], row=row_peer(j))

    track("e", e_all.at[pl.ds(0, NR - 1)], e_all.at[pl.ds(0, NR - 1)])

    land("s_yz")
    for n in range(NZ):
        s_all[n, k, x] = jnp.concatenate([s_rows[NY * n : NY * n + NY, i, :] for i in range(4)], axis=1)
    for i in (1, 3, 2):
        push("s_x", s_all.at[:, k, x], s_all.at[:, k, x], s_g.at[i], row=x_peer(i))
    track("s_x", s_all.at[:, 0, pl.ds(0, NX - 1)])
    push("s_p", s_all.at[:, k, x], s_all.at[:, k, x], col=partner)
    land("art_z")
    push("art_p", art.at[:, k], art.at[:, k], col=partner)
    track("art_p", art.at[:, 0], art.at[:, 0])
    for i in (1, 3, 2):
        origin = lax.rem(x + NX - i, NX)
        settle(s_all.at[:, k, origin], s_g.at[i])
        push("s_p", s_all.at[:, k, origin], s_all.at[:, k, origin], col=partner)
    track("s_p", s_all.at[:, 0], s_all.at[:, 0])
    land("s_p")

    eye = at == to
    innovation = s_all[...].reshape(512, 512) + jnp.where(eye, FORGET, 0.0)
    bound = jnp.max(jnp.sum(jnp.abs(innovation), axis=0, keepdims=True), axis=1, keepdims=True)
    land("art_p")
    power = split(jnp.where(eye, 1.0, 0.0) - innovation / bound)
    gain = art[...].reshape(512, 256) / bound
    gain = gain + dot3(power, gain, NORMAL)
    for step in range(2):
        power = split(dot3(power, power, NORMAL))
        gain = gain + dot3(power, gain, NORMAL)
    gain = gain + dot3(power, dot3(power, gain, NORMAL), NORMAL)
    gain_ref[...] = gain

    land("e")
    spread = (
        lax.broadcasted_iota(jnp.int32, (512, NR), 1)
        == lax.div(lax.broadcasted_iota(jnp.int32, (512, NR), 0), NC)
    ).astype(F32)
    errors = jnp.concatenate([e_all[n] for n in range(NR)], axis=0)
    picked = jnp.dot(spread, errors, precision=lax.Precision.HIGHEST)
    own_lane = lax.broadcasted_iota(jnp.int32, (512, 128), 1) == lax.rem(
        lax.broadcasted_iota(jnp.int32, (512, 128), 0), NC
    )
    column = jnp.sum(jnp.where(own_lane, picked, 0.0), axis=1, keepdims=True)
    delta = jnp.sum(gain * column, axis=0, keepdims=True)
    upper = lax.div(c, 8)
    delta = jnp.where(upper == 0, delta[:, :128], delta[:, 128:])
    moved = w_ref[pl.ds(2 * r + upper, 1), :] + delta
    moved = pltpu.roll(moved, 128 - 16 * lax.rem(c, 8), 1)
    weight_ref[...] = moved[:, :16]

    for h in range(2):

        @pl.when(jnp.logical_not(takes & (half == h)))
        def _():
            settle(act.at[h], act_x.at[h])

    @pl.when(jnp.logical_not(own_target))
    def _():
        settle(art.at[0, 0], send.at[GROUPS.index("act")])

    @pl.when(takes)
    def _():
        for i in range(3):
            settle(act.at[0], send.at[GROUPS.index("act_x")])

    drain()


def finish(gain_ref, act_ref, cov_ref, weight_ref, newcov_ref, new_weight_ref):
    update = dot3(gain_ref[...], act_ref[0], COLS)
    newcov_ref[...] = (cov_ref[...] - update) * (1.0 / FORGET)
    new_weight_ref[...] = weight_ref[...]


def on_device(
    atom_types, neighbor_ids, switching, environment, force_weights, targets,
    type_embed, layer_weight, out_weight, covariance,
):
    vmem = pl.BlockSpec(memory_space=pltpu.VMEM)
    V = pltpu.VMEM
    D = pltpu.SemaphoreType.DMA
    scratch = [
        V((256, 256), F32), V((256, 512), BF16), V((256, 512), BF16), V((512, 512), BF16),
        V((NR, 2, 128), F32), V((NC, 4, 128), F32), V((1, 1, 128), F32),
        V((NR, 2, 128), F32), V((NC, 4, 128), F32), V((NC, 1, 128), F32), V((NR, 1, 128), F32),
        V((NZ, 2, NR, 256), F32), V((NR, NC, 512), F32),
        V((NY, 2, NR, 256), F32), V((NC, NR, 256), F32), V((NZ, 2, NR, 256), F32),
        V((NR, 4, 128), F32), V((NR, 4, 128), F32), V((NZ * NY, 4, 128), F32), V((NZ, 2, NX, 8, 512), F32),
        D((len(GROUPS),)), D((len(GROUPS),)), D((NY,)), D((NY,)), D((NC,)), D((2,)), D((NX,)),
    ]
    gain, act, weight = pl.pallas_call(
        kernel,
        out_shape=(
            jax.ShapeDtypeStruct((512, 256), F32),
            jax.ShapeDtypeStruct((2, NC, NR, 256), F32),
            jax.ShapeDtypeStruct((1, 16), F32),
        ),
        in_specs=[vmem] * 10,
        out_specs=(vmem, vmem, vmem),
        scratch_shapes=scratch,
        compiler_params=pltpu.CompilerParams(
            collective_id=0, has_side_effects=True, vmem_limit_bytes=60 * 1024 * 1024
        ),
    )(
        atom_types, neighbor_ids[0], switching[0], environment[0].T, force_weights,
        targets.reshape(1, 1), type_embed, layer_weight, out_weight.reshape(1, 128), covariance,
    )
    new_cov, new_weight = pl.pallas_call(
        finish,
        grid=(2,),
        out_shape=(
            jax.ShapeDtypeStruct((256, 512), F32),
            jax.ShapeDtypeStruct((1, 16), F32),
        ),
        in_specs=[
            pl.BlockSpec((512, 256), lambda h: (0, 0)),
            pl.BlockSpec((1, 512, 256), lambda h: (h, 0, 0)),
            pl.BlockSpec((256, 256), lambda h: (0, h)),
            pl.BlockSpec((1, 16), lambda h: (0, 0)),
        ],
        out_specs=(
            pl.BlockSpec((256, 256), lambda h: (0, h)),
            pl.BlockSpec((1, 16), lambda h: (0, 0)),
        ),
    )(gain, act.reshape(2, 512, 256), covariance, weight)
    return (new_weight.reshape(16), new_cov)


def solution(mesh):
    in_specs = (
        P(("row", "col"), None),
        P(("row", "col"), None, None),
        P(("row", "col"), None, None),
        P(("row", "col"), None, None),
        P(("row", "col"), None),
        P(("row", "col")),
        P(),
        P(),
        P(),
        P("row", "col"),
    )
    out_specs = (P(("row", "col")), P("row", "col"))
    return jax.shard_map(
        on_device, mesh=mesh, in_specs=in_specs, out_specs=out_specs, check_vma=False
    )
```

```python
import functools
import itertools
import math

import jax
import jax.numpy as jnp
from jax import lax
from jax.experimental import pallas as pl
from jax.experimental.pallas import tpu as pltpu
from jax.sharding import PartitionSpec as P

FORGET = 0.98
MESH = pl.DeviceIdType.MESH
F32 = jnp.float32
BF16 = jnp.bfloat16
NX, NY, NZ = 4, 8, 8
NR, NC = 32, 16
NEAR = (1, 7, 2, 6, 3, 5, 4)


def far_first(*sizes):
    spots = [o for o in itertools.product(*map(range, sizes)) if any(o)]
    return sorted(spots, key=lambda o: -sum(min(d, n - d) for d, n in zip(o, sizes)))


GROUPS = (
    "jcol", "jrow", "err", "jc_y", "jc_x", "jr_z", "jr_p", "e", "w", "art_z", "art_p",
    "s", "s_yz", "s_x", "s_p", "act", "act_x",
)


def split(a):
    hi = a.astype(BF16)
    lo = (a - hi.astype(F32)).astype(BF16)
    return hi, lo


def mm(a, b, dims):
    return lax.dot_general(a, b, (dims, ((), ())), preferred_element_type=F32)


def dot3(a, b, dims):
    ah, al = a if isinstance(a, tuple) else split(a)
    bh, bl = b if isinstance(b, tuple) else split(b)
    return mm(ah, bh, dims) + (mm(ah, bl, dims) + mm(al, bh, dims))


ROWS = ((1,), (1,))
COLS = ((0,), (0,))
NORMAL = ((1,), (0,))


def kernel(
    types_ref, nbr_ref, sw_ref, env_ref, fw_ref, tgt_ref, te_ref, w_ref, ow_ref, cov_ref,
    gain_ref, act, weight_ref,
    select, cov_hi, cov_lo, order, jrow_send, jcol_send, e_send, jr_recv, jc_recv, e_recv, e_all,
    jr_all, jc_all, w_send, w_recv, art,
    s_send, s_recv, s_rows, s_all,
    send, recv, jc_y, jc_x, act_in, act_x, s_g,
):
    r = lax.axis_index("row")
    c = lax.axis_index("col")
    x, y = lax.rem(r, NX), lax.div(r, NX)
    k, z = lax.rem(c, 2), lax.div(c, 2)

    def row_peer(j):
        return lax.rem(r + j, NR)

    def col_peer(j):
        return lax.rem(c + j, NC)

    def x_peer(j):
        return y * NX + lax.rem(x + j, NX)

    def y_peer(j):
        return lax.rem(y + j, NY) * NX + x

    def z_peer(j):
        return lax.rem(z + j, NZ) * 2 + k

    partner = z * 2 + 1 - k
    flight = {}

    def push(name, src, dst, sem=None, **where):
        at = GROUPS.index(name)
        pltpu.make_async_remote_copy(
            src_ref=src, dst_ref=dst, send_sem=send.at[at],
            recv_sem=recv.at[at] if sem is None else sem,
            device_id=where, device_id_type=MESH,
        ).start()

    def settle(ref, sem):
        pltpu.make_async_copy(ref, ref, sem).wait()

    def track(name, sent, got=None):
        at = GROUPS.index(name)
        flight[name] = [(sent, send.at[at])]
        if got is not None:
            flight[name].append((got, recv.at[at]))

    def land(name):
        settle(*flight[name].pop())

    def drain():
        for waits in flight.values():
            for ref, sem in waits:
                settle(ref, sem)

    barrier = pltpu.get_barrier_semaphore()

    @pl.loop(1, NR)
    def _(j):
        pl.semaphore_signal(barrier, inc=1, device_id={"row": row_peer(j)}, device_id_type=MESH)

    @pl.loop(1, NC)
    def _(j):
        pl.semaphore_signal(barrier, inc=1, device_id={"col": col_peer(j)}, device_id_type=MESH)

    across = lax.div(r, 2)
    source = z * NX + x
    takes = lax.div(x, 2) == k
    half = lax.rem(x, 2)

    @pl.when(takes)
    def _():
        @pl.loop(0, NC)
        def _(p):
            @pl.when((source != r) | (p != c))
            def _():
                pl.semaphore_signal(
                    barrier, inc=1, device_id={"row": source, "col": p}, device_id_type=MESH
                )

    own_target = across == c

    block = 32

    @pl.loop(0, 256 // block)
    def _(b):
        ids = lax.broadcasted_iota(jnp.int32, (block, 256), 0) + b * block
        total = jnp.zeros((block, 256), F32)
        for n in range(32):
            total += jnp.where(ids == nbr_ref[n : n + 1, :], sw_ref[n : n + 1, :], 0.0)
        select[pl.ds(b * block, block), :] = total

    kinds = lax.broadcasted_iota(jnp.int32, (4, 256), 0)
    onehot = (kinds == types_ref[...]).astype(F32)
    mixed = env_ref[...] + dot3(te_ref[...], onehot, COLS)
    descriptor = dot3(mixed, select[...], NORMAL) / math.sqrt(32)
    hidden = jnp.tanh(descriptor)
    activity = jnp.tanh(dot3(hidden, w_ref[...], COLS))
    weighted = dot3(fw_ref[...], activity, NORMAL)
    scale = 1.0 / math.sqrt(256)
    predicted = jnp.sum(weighted * ow_ref[...], axis=1, keepdims=True) * scale
    error = tgt_ref[...] - predicted
    slopes = ow_ref[...] * (1.0 - activity * activity)
    jac = dot3(hidden * fw_ref[...], slopes, NORMAL) * scale

    for n in range(NC):
        jcol_send[n] = jac[4 * n : 4 * n + 4, :]
    for n in range(NR):
        jrow_send[n] = jac[2 * n : 2 * n + 2, :]
    e_send[0] = jnp.broadcast_to(error, (1, 128))
    cov_hi[...], cov_lo[...] = split(cov_ref[...])
    at = lax.broadcasted_iota(jnp.int32, (512, 512), 0)
    to = lax.broadcasted_iota(jnp.int32, (512, 512), 1)
    order[...] = (to == lax.rem(at, NC) * NR + lax.div(at, NC)).astype(F32).astype(BF16)

    pl.semaphore_wait(barrier, NR - 1 + NC - 1 + NY - own_target.astype(jnp.int32))

    zs = [lax.rem(z + d, NZ) * 2 for d in range(NZ)]
    ys = [lax.rem(y + d, NY) for d in range(NY)]
    xs = [lax.rem(x + d, NX) for d in range(NX)]
    for dz, dk in far_first(NZ, 2):
        p = zs[dz] + (k if dk == 0 else 1 - k)
        push("jcol", jcol_send.at[p], jc_recv.at[c], col=p)

    @pl.loop(1, NR)
    def _(j):
        p = row_peer(j)
        push("jrow", jrow_send.at[p], jr_recv.at[r], row=p)

    @pl.loop(1, NC)
    def _(j):
        push("err", e_send.at[0], e_recv.at[c], col=col_peer(j))

    track("jcol", jcol_send.at[pl.ds(0, NC - 1)], jc_recv.at[pl.ds(0, NC - 1)])
    track("jrow", jrow_send.at[pl.ds(0, NR - 1)], jr_recv.at[pl.ds(0, NR - 1)])
    track("err", e_recv.at[pl.ds(0, NC - 1)], e_recv.at[pl.ds(0, NC - 1)])
    jc_recv[c] = jcol_send[c]
    jr_recv[r] = jrow_send[r]
    e_recv[c] = e_send[0]

    land("jcol")
    jc_all[r] = jnp.concatenate([jc_recv[:, n, :] for n in range(4)], axis=1)

    for j in NEAR:
        push("jc_y", jc_all.at[r], jc_all.at[r], jc_y.at[j], row=y_peer(j))
    for i in (1, 3, 2):
        push("jc_x", jc_all.at[r], jc_all.at[r], jc_x.at[0], row=x_peer(i))
    track("jc_y", jc_all.at[pl.ds(0, NY - 1)])
    track("jc_x", jc_all.at[pl.ds(0, NR - NY)])

    land("jrow")
    jr_all[z, k] = jnp.concatenate([jr_recv[:, n, :] for n in range(2)], axis=1)
    for j in NEAR:
        push("jr_z", jr_all.at[z, k], jr_all.at[z, k], col=z_peer(j))
    track("jr_z", jr_all.at[pl.ds(0, NZ - 1), 0], jr_all.at[pl.ds(0, NZ - 1), 0])

    def pass_jc(j):
        slot = y_peer(NY - j)
        settle(jc_all.at[slot], jc_y.at[j])
        for i in (1, 3, 2):
            push("jc_x", jc_all.at[slot], jc_all.at[slot], jc_x.at[j], row=x_peer(i))

    cov = (cov_hi[...], cov_lo[...])
    for j in NEAR[:3]:
        pass_jc(j)
    for n, j in enumerate((0,) + NEAR):
        there = lax.rem(y + NY - j, NY)
        settle(jc_all.at[pl.ds(0, NX - 1)], jc_x.at[j])
        part = dot3(jc_all[pl.ds(there * NX, NX)].reshape(64, 512), cov, ROWS)
        w_send[there] = part.reshape(2, NR, 256)
        for h in range(2):

            @pl.when(2 * there + h != c)
            def _():
                push("w", w_send.at[there, h], w_recv.at[c], col=2 * there + h)

            @pl.when(2 * there + h == c)
            def _():
                w_recv[c] = w_send[there, h]

        if n + 3 < len(NEAR):
            pass_jc(NEAR[n + 3])
        if n == 5:
            land("jr_z")
            push("jr_p", jr_all.at[:, k], jr_all.at[:, k], col=partner)
            track("jr_p", jr_all.at[:, 0], jr_all.at[:, 0])
    track("w", w_recv.at[pl.ds(0, NC - 1)], w_recv.at[pl.ds(0, NC - 1)])

    land("err")
    lanes = lax.broadcasted_iota(jnp.int32, (NC, 128), 1)
    spots = lax.broadcasted_iota(jnp.int32, (NC, 128), 0)
    e_all[r] = jnp.sum(jnp.where(lanes == spots, e_recv[:, 0, :], 0.0), axis=0, keepdims=True)

    land("jr_p")
    jh, jl = split(jr_all[...].reshape(512, 256))
    perm = order[...]
    jr = (mm(perm, jh, NORMAL).astype(BF16), mm(perm, jl, NORMAL).astype(BF16))

    land("w")
    own = jnp.sum(w_recv[...], axis=0)
    art[z, k] = own

    s_part = dot3(own, jr, ROWS)
    for n in range(4):
        s_send[:, n, :] = s_part[:, 128 * n : 128 * n + 128]

    for dy, dx in far_first(NY, NX):
        push("s", s_send.at[xs[dx] * NY + ys[dy]], s_recv.at[r], row=ys[dy] * NX + xs[dx])

    track("s", s_send.at[pl.ds(0, NR - 1)], s_recv.at[pl.ds(0, NR - 1)])
    s_recv[r] = s_send[x * NY + y]

    for j in (0,) + NEAR:
        to_row = y_peer(j)
        if j == 0:

            @pl.when(jnp.logical_not(own_target))
            def _():
                push("act", art.at[z, k], act.at[half, c], act_in.at[c], row=to_row, col=across)

            @pl.when(own_target)
            def _():
                act[half, c] = own

        else:
            push("act", art.at[z, k], act.at[half, c], act_in.at[c], row=to_row, col=across)
    track("act", art.at[pl.ds(0, NY - 1), 0])

    land("s")
    spot = z * NY + y
    s_rows[spot] = jnp.sum(s_recv[...], axis=0)

    for dy, dz in far_first(NY, NZ):
        push("s_yz", s_rows.at[spot], s_rows.at[spot], row=ys[dy] * NX + x, col=zs[dz] + k)

    most = s_rows.at[pl.ds(0, NY * NZ - 1)]
    track("s_yz", most, most)

    for j in NEAR:
        push("art_z", art.at[z, k], art.at[z, k], col=z_peer(j))
    track("art_z", art.at[pl.ds(0, NZ - 1), 0], art.at[pl.ds(0, NZ - 1), 0])

    @pl.when(takes)
    def _():
        for j in (0, 1, 7, 2, 6, 3, 5, 4):
            for h in range(2):
                p = lax.rem(z + j, NZ) * 2 + h

                @pl.when((source != r) | (p != c))
                def _():
                    settle(act.at[half, p], act_in.at[p])

                for i in (1, 3, 2):
                    push("act_x", act.at[half, p], act.at[half, p], act_x.at[half], row=x_peer(i))

    @pl.loop(1, NR)
    def _(j):
        push("e", e_all.at[r], e_all.at[r], row=row_peer(j))

    track("e", e_all.at[pl.ds(0, NR - 1)], e_all.at[pl.ds(0, NR - 1)])

    land("s_yz")
    for n in range(NZ):
        s_all[n, k, x] = jnp.concatenate([s_rows[NY * n : NY * n + NY, i, :] for i in range(4)], axis=1)
    for i in (1, 3, 2):
        push("s_x", s_all.at[:, k, x], s_all.at[:, k, x], s_g.at[i], row=x_peer(i))
    track("s_x", s_all.at[:, 0, pl.ds(0, NX - 1)])
    push("s_p", s_all.at[:, k, x], s_all.at[:, k, x], col=partner)
    land("art_z")
    push("art_p", art.at[:, k], art.at[:, k], col=partner)
    track("art_p", art.at[:, 0], art.at[:, 0])
    for i in (1, 3, 2):
        origin = lax.rem(x + NX - i, NX)
        settle(s_all.at[:, k, origin], s_g.at[i])
        push("s_p", s_all.at[:, k, origin], s_all.at[:, k, origin], col=partner)
    track("s_p", s_all.at[:, 0], s_all.at[:, 0])

    land("e")
    spread = (
        lax.broadcasted_iota(jnp.int32, (512, NR), 1)
        == lax.div(lax.broadcasted_iota(jnp.int32, (512, NR), 0), NC)
    ).astype(F32)
    errors = jnp.concatenate([e_all[n] for n in range(NR)], axis=0)
    picked = jnp.dot(spread, errors, precision=lax.Precision.HIGHEST)
    own_lane = lax.broadcasted_iota(jnp.int32, (512, 128), 1) == lax.rem(
        lax.broadcasted_iota(jnp.int32, (512, 128), 0), NC
    )
    errors = dot3(jnp.ones((8, 128), F32), jnp.where(own_lane, picked, 0.0), ROWS)
    land("art_p")
    products = art[...].reshape(512, 256).T
    land("s_p")

    eye = at == to
    innovation = s_all[...].reshape(512, 512) + jnp.where(eye, FORGET, 0.0)
    bound = jnp.max(jnp.sum(jnp.abs(innovation), axis=0, keepdims=True), axis=1, keepdims=True)
    ph, pw = split(jnp.where(eye, 1.0, 0.0) - innovation / bound)
    gain = products / bound
    for step in range(2):
        gh, gl = split(gain)
        first = mm(jnp.concatenate([ph, gh, gl], axis=0), ph, NORMAL)
        second = mm(jnp.concatenate([ph, gh], axis=0), pw, NORMAL)
        mixed = second[:512]
        gain = gain + (first[512:768] + (first[768:] + second[512:]))
        ph, pw = split(first[:512] + (mixed + mixed.T))
    power = (ph, pw)
    gain = gain + dot3(gain, power, NORMAL)
    gain = gain + dot3(dot3(gain, power, NORMAL), power, NORMAL)
    gain_ref[...] = gain

    delta = dot3(errors, gain, ROWS)[:1]
    upper = lax.div(c, 8)
    delta = jnp.where(upper == 0, delta[:, :128], delta[:, 128:])
    moved = w_ref[pl.ds(2 * r + upper, 1), :] + delta
    moved = pltpu.roll(moved, 128 - 16 * lax.rem(c, 8), 1)
    weight_ref[...] = moved[:, :16]

    for h in range(2):

        @pl.when(jnp.logical_not(takes & (half == h)))
        def _():
            settle(act.at[h], act_x.at[h])

    @pl.when(jnp.logical_not(own_target))
    def _():
        settle(art.at[0, 0], send.at[GROUPS.index("act")])

    @pl.when(takes)
    def _():
        for i in range(3):
            settle(act.at[0], send.at[GROUPS.index("act_x")])

    drain()


def finish(gain_ref, act_ref, cov_ref, weight_ref, newcov_ref, new_weight_ref):
    update = dot3(gain_ref[...], act_ref[0], NORMAL)
    newcov_ref[...] = (cov_ref[...] - update) * (1.0 / FORGET)
    new_weight_ref[...] = weight_ref[...]


def on_device(
    atom_types, neighbor_ids, switching, environment, force_weights, targets,
    type_embed, layer_weight, out_weight, covariance,
):
    vmem = pl.BlockSpec(memory_space=pltpu.VMEM)
    V = pltpu.VMEM
    D = pltpu.SemaphoreType.DMA
    scratch = [
        V((256, 256), F32), V((256, 512), BF16), V((256, 512), BF16), V((512, 512), BF16),
        V((NR, 2, 128), F32), V((NC, 4, 128), F32), V((1, 1, 128), F32),
        V((NR, 2, 128), F32), V((NC, 4, 128), F32), V((NC, 1, 128), F32), V((NR, 1, 128), F32),
        V((NZ, 2, NR, 256), F32), V((NR, NC, 512), F32),
        V((NY, 2, NR, 256), F32), V((NC, NR, 256), F32), V((NZ, 2, NR, 256), F32),
        V((NR, 4, 128), F32), V((NR, 4, 128), F32), V((NZ * NY, 4, 128), F32), V((NZ, 2, NX, 8, 512), F32),
        D((len(GROUPS),)), D((len(GROUPS),)), D((NY,)), D((NY,)), D((NC,)), D((2,)), D((NX,)),
    ]
    gain, act, weight = pl.pallas_call(
        kernel,
        out_shape=(
            jax.ShapeDtypeStruct((256, 512), F32),
            jax.ShapeDtypeStruct((2, NC, NR, 256), F32),
            jax.ShapeDtypeStruct((1, 16), F32),
        ),
        in_specs=[vmem] * 10,
        out_specs=(vmem, vmem, vmem),
        scratch_shapes=scratch,
        compiler_params=pltpu.CompilerParams(
            collective_id=0, has_side_effects=True, vmem_limit_bytes=60 * 1024 * 1024
        ),
    )(
        atom_types, neighbor_ids[0], switching[0], environment[0].T, force_weights,
        targets.reshape(1, 1), type_embed, layer_weight, out_weight.reshape(1, 128), covariance,
    )
    new_cov, new_weight = pl.pallas_call(
        finish,
        grid=(2,),
        out_shape=(
            jax.ShapeDtypeStruct((256, 512), F32),
            jax.ShapeDtypeStruct((1, 16), F32),
        ),
        in_specs=[
            pl.BlockSpec((256, 512), lambda h: (0, 0)),
            pl.BlockSpec((1, 512, 256), lambda h: (h, 0, 0)),
            pl.BlockSpec((256, 256), lambda h: (0, h)),
            pl.BlockSpec((1, 16), lambda h: (0, 0)),
        ],
        out_specs=(
            pl.BlockSpec((256, 256), lambda h: (0, h)),
            pl.BlockSpec((1, 16), lambda h: (0, 0)),
        ),
    )(gain, act.reshape(2, 512, 256), covariance, weight)
    return (new_weight.reshape(16), new_cov)


def solution(mesh):
    in_specs = (
        P(("row", "col"), None),
        P(("row", "col"), None, None),
        P(("row", "col"), None, None),
        P(("row", "col"), None, None),
        P(("row", "col"), None),
        P(("row", "col")),
        P(),
        P(),
        P(),
        P("row", "col"),
    )
    out_specs = (P(("row", "col")), P("row", "col"))
    return jax.shard_map(
        on_device, mesh=mesh, in_specs=in_specs, out_specs=out_specs, check_vma=False
    )
```

```python
import functools
import itertools
import math

import jax
import jax.numpy as jnp
from jax import lax
from jax.experimental import pallas as pl
from jax.experimental.pallas import tpu as pltpu
from jax.sharding import PartitionSpec as P

FORGET = 0.98
MESH = pl.DeviceIdType.MESH
F32 = jnp.float32
BF16 = jnp.bfloat16
NX, NY, NZ = 4, 8, 8
NR, NC = 32, 16
NEAR = (1, 7, 2, 6, 3, 5, 4)


def far_first(*sizes):
    spots = [o for o in itertools.product(*map(range, sizes)) if any(o)]
    return sorted(spots, key=lambda o: -sum(min(d, n - d) for d, n in zip(o, sizes)))


GROUPS = (
    "jcol", "jrow", "err", "jc_y", "jc_x", "jr_z", "jr_p", "e", "w", "art_z", "art_p",
    "s", "s_yz", "s_x", "s_p", "act", "act_x",
)


def split(a):
    hi = a.astype(BF16)
    lo = (a - hi.astype(F32)).astype(BF16)
    return hi, lo


def mm(a, b, dims):
    return lax.dot_general(a, b, (dims, ((), ())), preferred_element_type=F32)


def dot3(a, b, dims):
    ah, al = a if isinstance(a, tuple) else split(a)
    bh, bl = b if isinstance(b, tuple) else split(b)
    return mm(ah, bh, dims) + (mm(ah, bl, dims) + mm(al, bh, dims))


ROWS = ((1,), (1,))
COLS = ((0,), (0,))
NORMAL = ((1,), (0,))


def kernel(
    types_ref, nbr_ref, sw_ref, env_ref, fw_ref, tgt_ref, te_ref, w_ref, ow_ref, cov_ref,
    gain_ref, act, weight_ref,
    select, cov_hi, cov_lo, order, jrow_send, jcol_send, e_send, jr_recv, jc_recv, e_recv, e_all,
    jr_all, jc_all, w_send, w_recv, art,
    s_send, s_recv, s_rows, s_all,
    send, recv, jc_y, jc_x, act_in, act_x, s_z, s_g,
):
    r = lax.axis_index("row")
    c = lax.axis_index("col")
    x, y = lax.rem(r, NX), lax.div(r, NX)
    k, z = lax.rem(c, 2), lax.div(c, 2)

    def row_peer(j):
        return lax.rem(r + j, NR)

    def col_peer(j):
        return lax.rem(c + j, NC)

    def x_peer(j):
        return y * NX + lax.rem(x + j, NX)

    def y_peer(j):
        return lax.rem(y + j, NY) * NX + x

    def z_peer(j):
        return lax.rem(z + j, NZ) * 2 + k

    partner = z * 2 + 1 - k
    flight = {}

    def push(name, src, dst, sem=None, **where):
        at = GROUPS.index(name)
        pltpu.make_async_remote_copy(
            src_ref=src, dst_ref=dst, send_sem=send.at[at],
            recv_sem=recv.at[at] if sem is None else sem,
            device_id=where, device_id_type=MESH,
        ).start()

    def settle(ref, sem):
        pltpu.make_async_copy(ref, ref, sem).wait()

    def track(name, sent, got=None):
        at = GROUPS.index(name)
        flight[name] = [(sent, send.at[at])]
        if got is not None:
            flight[name].append((got, recv.at[at]))

    def land(name):
        settle(*flight[name].pop())

    def drain():
        for waits in flight.values():
            for ref, sem in waits:
                settle(ref, sem)

    barrier = pltpu.get_barrier_semaphore()

    @pl.loop(1, NR)
    def _(j):
        pl.semaphore_signal(barrier, inc=1, device_id={"row": row_peer(j)}, device_id_type=MESH)

    @pl.loop(1, NC)
    def _(j):
        pl.semaphore_signal(barrier, inc=1, device_id={"col": col_peer(j)}, device_id_type=MESH)

    across = lax.div(r, 2)
    source = z * NX + x
    takes = lax.div(x, 2) == k
    half = lax.rem(x, 2)

    @pl.when(takes)
    def _():
        @pl.loop(0, NC)
        def _(p):
            @pl.when((source != r) | (p != c))
            def _():
                pl.semaphore_signal(
                    barrier, inc=1, device_id={"row": source, "col": p}, device_id_type=MESH
                )

    own_target = across == c

    block = 32

    @pl.loop(0, 256 // block)
    def _(b):
        ids = lax.broadcasted_iota(jnp.int32, (block, 256), 0) + b * block
        total = jnp.zeros((block, 256), F32)
        for n in range(32):
            total += jnp.where(ids == nbr_ref[n : n + 1, :], sw_ref[n : n + 1, :], 0.0)
        select[pl.ds(b * block, block), :] = total

    kinds = lax.broadcasted_iota(jnp.int32, (4, 256), 0)
    onehot = (kinds == types_ref[...]).astype(F32)
    mixed = env_ref[...] + dot3(te_ref[...], onehot, COLS)
    descriptor = dot3(mixed, select[...], NORMAL) / math.sqrt(32)
    hidden = jnp.tanh(descriptor)
    activity = jnp.tanh(dot3(hidden, w_ref[...], COLS))
    weighted = dot3(fw_ref[...], activity, NORMAL)
    scale = 1.0 / math.sqrt(256)
    predicted = jnp.sum(weighted * ow_ref[...], axis=1, keepdims=True) * scale
    error = tgt_ref[...] - predicted
    slopes = ow_ref[...] * (1.0 - activity * activity)
    jac = dot3(hidden * fw_ref[...], slopes, NORMAL) * scale

    for n in range(NC):
        jcol_send[n] = jac[4 * n : 4 * n + 4, :]
    for n in range(NR):
        jrow_send[n] = jac[2 * n : 2 * n + 2, :]
    e_send[0] = jnp.broadcast_to(error, (1, 128))
    cov_hi[...], cov_lo[...] = split(cov_ref[...])
    at = lax.broadcasted_iota(jnp.int32, (512, 512), 0)
    to = lax.broadcasted_iota(jnp.int32, (512, 512), 1)
    order[...] = (to == lax.rem(at, NC) * NR + lax.div(at, NC)).astype(F32).astype(BF16)

    pl.semaphore_wait(barrier, NR - 1 + NC - 1 + NY - own_target.astype(jnp.int32))

    zs = [lax.rem(z + d, NZ) * 2 for d in range(NZ)]
    ys = [lax.rem(y + d, NY) for d in range(NY)]
    xs = [lax.rem(x + d, NX) for d in range(NX)]
    for dz, dk in far_first(NZ, 2):
        p = zs[dz] + (k if dk == 0 else 1 - k)
        push("jcol", jcol_send.at[p], jc_recv.at[c], col=p)

    @pl.loop(1, NR)
    def _(j):
        p = row_peer(j)
        push("jrow", jrow_send.at[p], jr_recv.at[r], row=p)

    @pl.loop(1, NC)
    def _(j):
        push("err", e_send.at[0], e_recv.at[c], col=col_peer(j))

    track("jcol", jcol_send.at[pl.ds(0, NC - 1)], jc_recv.at[pl.ds(0, NC - 1)])
    track("jrow", jrow_send.at[pl.ds(0, NR - 1)], jr_recv.at[pl.ds(0, NR - 1)])
    track("err", e_recv.at[pl.ds(0, NC - 1)], e_recv.at[pl.ds(0, NC - 1)])
    jc_recv[c] = jcol_send[c]
    jr_recv[r] = jrow_send[r]
    e_recv[c] = e_send[0]

    land("jcol")
    jc_all[r] = jnp.concatenate([jc_recv[:, n, :] for n in range(4)], axis=1)

    for j in NEAR:
        push("jc_y", jc_all.at[r], jc_all.at[r], jc_y.at[j], row=y_peer(j))
    for i in (1, 3, 2):
        push("jc_x", jc_all.at[r], jc_all.at[r], jc_x.at[0], row=x_peer(i))
    track("jc_y", jc_all.at[pl.ds(0, NY - 1)])
    track("jc_x", jc_all.at[pl.ds(0, NR - NY)])

    land("jrow")
    jr_all[z, k] = jnp.concatenate([jr_recv[:, n, :] for n in range(2)], axis=1)
    for j in NEAR:
        push("jr_z", jr_all.at[z, k], jr_all.at[z, k], col=z_peer(j))
    track("jr_z", jr_all.at[pl.ds(0, NZ - 1), 0], jr_all.at[pl.ds(0, NZ - 1), 0])

    def pass_jc(j):
        slot = y_peer(NY - j)
        settle(jc_all.at[slot], jc_y.at[j])
        for i in (1, 3, 2):
            push("jc_x", jc_all.at[slot], jc_all.at[slot], jc_x.at[j], row=x_peer(i))

    cov = (cov_hi[...], cov_lo[...])
    for j in NEAR[:3]:
        pass_jc(j)
    for n, j in enumerate((0,) + NEAR):
        there = lax.rem(y + NY - j, NY)
        settle(jc_all.at[pl.ds(0, NX - 1)], jc_x.at[j])
        part = dot3(jc_all[pl.ds(there * NX, NX)].reshape(64, 512), cov, ROWS)
        w_send[there] = part.reshape(2, NR, 256)
        for h in range(2):

            @pl.when(2 * there + h != c)
            def _():
                push("w", w_send.at[there, h], w_recv.at[c], col=2 * there + h)

            @pl.when(2 * there + h == c)
            def _():
                w_recv[c] = w_send[there, h]

        if n + 3 < len(NEAR):
            pass_jc(NEAR[n + 3])
        if n == 5:
            land("jr_z")
            push("jr_p", jr_all.at[:, k], jr_all.at[:, k], col=partner)
            track("jr_p", jr_all.at[:, 0], jr_all.at[:, 0])
    track("w", w_recv.at[pl.ds(0, NC - 1)], w_recv.at[pl.ds(0, NC - 1)])

    land("err")
    lanes = lax.broadcasted_iota(jnp.int32, (NC, 128), 1)
    spots = lax.broadcasted_iota(jnp.int32, (NC, 128), 0)
    e_all[r] = jnp.sum(jnp.where(lanes == spots, e_recv[:, 0, :], 0.0), axis=0, keepdims=True)

    land("jr_p")
    jh, jl = split(jr_all[...].reshape(512, 256))
    perm = order[...]
    jr = (mm(perm, jh, NORMAL).astype(BF16), mm(perm, jl, NORMAL).astype(BF16))

    land("w")
    own = jnp.sum(w_recv[...], axis=0)
    art[z, k] = own

    s_part = dot3(own, jr, ROWS)
    for n in range(4):
        s_send[:, n, :] = s_part[:, 128 * n : 128 * n + 128]

    for dy, dx in far_first(NY, NX):
        push("s", s_send.at[xs[dx] * NY + ys[dy]], s_recv.at[r], row=ys[dy] * NX + xs[dx])

    track("s", s_send.at[pl.ds(0, NR - 1)], s_recv.at[pl.ds(0, NR - 1)])
    s_recv[r] = s_send[x * NY + y]

    for j in (0,) + NEAR:
        to_row = y_peer(j)
        if j == 0:

            @pl.when(jnp.logical_not(own_target))
            def _():
                push("act", art.at[z, k], act.at[half, c], act_in.at[c], row=to_row, col=across)

            @pl.when(own_target)
            def _():
                act[half, c] = own

        else:
            push("act", art.at[z, k], act.at[half, c], act_in.at[c], row=to_row, col=across)
    track("act", art.at[pl.ds(0, NY - 1), 0])

    land("s")
    spot = z * NY + y
    s_rows[spot] = jnp.sum(s_recv[...], axis=0)

    for dy, dz in far_first(NY, NZ):
        push("s_yz", s_rows.at[spot], s_rows.at[spot], s_z.at[dz], row=ys[dy] * NX + x, col=zs[dz] + k)

    track("s_yz", s_rows.at[pl.ds(0, NY * NZ - 1)])

    for j in NEAR:
        push("art_z", art.at[z, k], art.at[z, k], col=z_peer(j))
    track("art_z", art.at[pl.ds(0, NZ - 1), 0], art.at[pl.ds(0, NZ - 1), 0])

    @pl.when(takes)
    def _():
        for j in (0, 1, 7, 2, 6, 3, 5, 4):
            for h in range(2):
                p = lax.rem(z + j, NZ) * 2 + h

                @pl.when((source != r) | (p != c))
                def _():
                    settle(act.at[half, p], act_in.at[p])

                for i in (1, 3, 2):
                    push("act_x", act.at[half, p], act.at[half, p], act_x.at[half], row=x_peer(i))

    @pl.loop(1, NR)
    def _(j):
        push("e", e_all.at[r], e_all.at[r], row=row_peer(j))

    track("e", e_all.at[pl.ds(0, NR - 1)], e_all.at[pl.ds(0, NR - 1)])

    for dz in (0,) + NEAR:
        n = lax.rem(z + NZ - dz, NZ)
        settle(s_rows.at[pl.ds(0, NY if dz else NY - 1)], s_z.at[dz])
        rows = s_rows[pl.ds(n * NY, NY)]
        s_all[n, k, x] = jnp.concatenate([rows[:, i, :] for i in range(4)], axis=1)
        for i in (1, 3, 2):
            push("s_x", s_all.at[n, k, x], s_all.at[n, k, x], s_g.at[i], row=x_peer(i))
    track("s_x", s_all.at[:, 0, pl.ds(0, NX - 1)])
    push("s_p", s_all.at[:, k, x], s_all.at[:, k, x], col=partner)
    land("art_z")
    push("art_p", art.at[:, k], art.at[:, k], col=partner)
    track("art_p", art.at[:, 0], art.at[:, 0])
    for i in (1, 3, 2):
        origin = lax.rem(x + NX - i, NX)
        settle(s_all.at[:, k, origin], s_g.at[i])
        push("s_p", s_all.at[:, k, origin], s_all.at[:, k, origin], col=partner)
    track("s_p", s_all.at[:, 0], s_all.at[:, 0])

    land("e")
    spread = (
        lax.broadcasted_iota(jnp.int32, (512, NR), 1)
        == lax.div(lax.broadcasted_iota(jnp.int32, (512, NR), 0), NC)
    ).astype(F32)
    errors = jnp.concatenate([e_all[n] for n in range(NR)], axis=0)
    picked = jnp.dot(spread, errors, precision=lax.Precision.HIGHEST)
    own_lane = lax.broadcasted_iota(jnp.int32, (512, 128), 1) == lax.rem(
        lax.broadcasted_iota(jnp.int32, (512, 128), 0), NC
    )
    errors = dot3(jnp.ones((8, 128), F32), jnp.where(own_lane, picked, 0.0), ROWS)
    land("art_p")
    products = art[...].reshape(512, 256).T
    land("s_p")

    eye = at == to
    innovation = s_all[...].reshape(512, 512) + jnp.where(eye, FORGET, 0.0)
    bound = jnp.max(jnp.sum(jnp.abs(innovation), axis=0, keepdims=True), axis=1, keepdims=True)
    ph, pw = split(jnp.where(eye, 1.0, 0.0) - innovation / bound)
    gain = products / bound
    for step in range(2):
        gh, gl = split(gain)
        first = mm(jnp.concatenate([ph, gh, gl], axis=0), ph, NORMAL)
        second = mm(jnp.concatenate([ph, gh], axis=0), pw, NORMAL)
        mixed = second[:512]
        gain = gain + (first[512:768] + (first[768:] + second[512:]))
        ph, pw = split(first[:512] + (mixed + mixed.T))
    power = (ph, pw)
    gain = gain + dot3(gain, power, NORMAL)
    gain = gain + dot3(dot3(gain, power, NORMAL), power, NORMAL)
    gain_ref[...] = gain

    delta = dot3(errors, gain, ROWS)[:1]
    upper = lax.div(c, 8)
    delta = jnp.where(upper == 0, delta[:, :128], delta[:, 128:])
    moved = w_ref[pl.ds(2 * r + upper, 1), :] + delta
    moved = pltpu.roll(moved, 128 - 16 * lax.rem(c, 8), 1)
    weight_ref[...] = moved[:, :16]

    for h in range(2):

        @pl.when(jnp.logical_not(takes & (half == h)))
        def _():
            settle(act.at[h], act_x.at[h])

    @pl.when(jnp.logical_not(own_target))
    def _():
        settle(art.at[0, 0], send.at[GROUPS.index("act")])

    @pl.when(takes)
    def _():
        for i in range(3):
            settle(act.at[0], send.at[GROUPS.index("act_x")])

    drain()


def finish(gain_ref, act_ref, cov_ref, weight_ref, newcov_ref, new_weight_ref):
    update = dot3(gain_ref[...], act_ref[0], NORMAL)
    newcov_ref[...] = (cov_ref[...] - update) * (1.0 / FORGET)
    new_weight_ref[...] = weight_ref[...]


def on_device(
    atom_types, neighbor_ids, switching, environment, force_weights, targets,
    type_embed, layer_weight, out_weight, covariance,
):
    vmem = pl.BlockSpec(memory_space=pltpu.VMEM)
    V = pltpu.VMEM
    D = pltpu.SemaphoreType.DMA
    scratch = [
        V((256, 256), F32), V((256, 512), BF16), V((256, 512), BF16), V((512, 512), BF16),
        V((NR, 2, 128), F32), V((NC, 4, 128), F32), V((1, 1, 128), F32),
        V((NR, 2, 128), F32), V((NC, 4, 128), F32), V((NC, 1, 128), F32), V((NR, 1, 128), F32),
        V((NZ, 2, NR, 256), F32), V((NR, NC, 512), F32),
        V((NY, 2, NR, 256), F32), V((NC, NR, 256), F32), V((NZ, 2, NR, 256), F32),
        V((NR, 4, 128), F32), V((NR, 4, 128), F32), V((NZ * NY, 4, 128), F32), V((NZ, 2, NX, 8, 512), F32),
        D((len(GROUPS),)), D((len(GROUPS),)), D((NY,)), D((NY,)), D((NC,)), D((2,)), D((NZ,)), D((NX,)),
    ]
    gain, act, weight = pl.pallas_call(
        kernel,
        out_shape=(
            jax.ShapeDtypeStruct((256, 512), F32),
            jax.ShapeDtypeStruct((2, NC, NR, 256), F32),
            jax.ShapeDtypeStruct((1, 16), F32),
        ),
        in_specs=[vmem] * 10,
        out_specs=(vmem, vmem, vmem),
        scratch_shapes=scratch,
        compiler_params=pltpu.CompilerParams(
            collective_id=0, has_side_effects=True, vmem_limit_bytes=60 * 1024 * 1024
        ),
    )(
        atom_types, neighbor_ids[0], switching[0], environment[0].T, force_weights,
        targets.reshape(1, 1), type_embed, layer_weight, out_weight.reshape(1, 128), covariance,
    )
    new_cov, new_weight = pl.pallas_call(
        finish,
        grid=(2,),
        out_shape=(
            jax.ShapeDtypeStruct((256, 512), F32),
            jax.ShapeDtypeStruct((1, 16), F32),
        ),
        in_specs=[
            pl.BlockSpec((256, 512), lambda h: (0, 0)),
            pl.BlockSpec((1, 512, 256), lambda h: (h, 0, 0)),
            pl.BlockSpec((256, 256), lambda h: (0, h)),
            pl.BlockSpec((1, 16), lambda h: (0, 0)),
        ],
        out_specs=(
            pl.BlockSpec((256, 256), lambda h: (0, h)),
            pl.BlockSpec((1, 16), lambda h: (0, 0)),
        ),
    )(gain, act.reshape(2, 512, 256), covariance, weight)
    return (new_weight.reshape(16), new_cov)


def solution(mesh):
    in_specs = (
        P(("row", "col"), None),
        P(("row", "col"), None, None),
        P(("row", "col"), None, None),
        P(("row", "col"), None, None),
        P(("row", "col"), None),
        P(("row", "col")),
        P(),
        P(),
        P(),
        P("row", "col"),
    )
    out_specs = (P(("row", "col")), P("row", "col"))
    return jax.shard_map(
        on_device, mesh=mesh, in_specs=in_specs, out_specs=out_specs, check_vma=False
    )
```

```python
import functools
import itertools
import math

import jax
import jax.numpy as jnp
from jax import lax
from jax.experimental import pallas as pl
from jax.experimental.pallas import tpu as pltpu
from jax.sharding import PartitionSpec as P

FORGET = 0.98
MESH = pl.DeviceIdType.MESH
F32 = jnp.float32
BF16 = jnp.bfloat16
NX, NY, NZ = 4, 8, 8
NR, NC = 32, 16
NEAR = (1, 7, 2, 6, 3, 5, 4)


def far_first(*sizes):
    spots = [o for o in itertools.product(*map(range, sizes)) if any(o)]
    return sorted(spots, key=lambda o: -sum(min(d, n - d) for d, n in zip(o, sizes)))


GROUPS = (
    "jcol", "jrow", "err", "jc_y", "jc_x", "jr_z", "jr_p", "e", "w", "art_z", "art_p",
    "s", "s_yz", "s_x", "s_p", "act", "act_x",
)


def split(a):
    hi = a.astype(BF16)
    lo = (a - hi.astype(F32)).astype(BF16)
    return hi, lo


def mm(a, b, dims):
    return lax.dot_general(a, b, (dims, ((), ())), preferred_element_type=F32)


def dot3(a, b, dims):
    ah, al = a if isinstance(a, tuple) else split(a)
    bh, bl = b if isinstance(b, tuple) else split(b)
    return mm(ah, bh, dims) + (mm(ah, bl, dims) + mm(al, bh, dims))


ROWS = ((1,), (1,))
COLS = ((0,), (0,))
NORMAL = ((1,), (0,))


def kernel(
    types_ref, nbr_ref, sw_ref, env_ref, fw_ref, tgt_ref, te_ref, w_ref, ow_ref, cov_ref,
    gain_ref, act, weight_ref,
    select, cov_hi, cov_lo, order, jrow_send, jcol_send, e_send, jr_recv, jc_recv, e_recv, e_all,
    jr_all, jc_all, w_send, w_recv, art,
    s_send, s_recv, s_rows, s_all,
    send, recv, jc_y, jc_x, act_in, act_x, s_g,
):
    r = lax.axis_index("row")
    c = lax.axis_index("col")
    x, y = lax.rem(r, NX), lax.div(r, NX)
    k, z = lax.rem(c, 2), lax.div(c, 2)

    def row_peer(j):
        return lax.rem(r + j, NR)

    def col_peer(j):
        return lax.rem(c + j, NC)

    def x_peer(j):
        return y * NX + lax.rem(x + j, NX)

    def y_peer(j):
        return lax.rem(y + j, NY) * NX + x

    def z_peer(j):
        return lax.rem(z + j, NZ) * 2 + k

    partner = z * 2 + 1 - k
    flight = {}

    def push(name, src, dst, sem=None, **where):
        at = GROUPS.index(name)
        pltpu.make_async_remote_copy(
            src_ref=src, dst_ref=dst, send_sem=send.at[at],
            recv_sem=recv.at[at] if sem is None else sem,
            device_id=where, device_id_type=MESH,
        ).start()

    def settle(ref, sem):
        pltpu.make_async_copy(ref, ref, sem).wait()

    def track(name, sent, got=None):
        at = GROUPS.index(name)
        flight[name] = [(sent, send.at[at])]
        if got is not None:
            flight[name].append((got, recv.at[at]))

    def land(name):
        settle(*flight[name].pop())

    def drain():
        for waits in flight.values():
            for ref, sem in waits:
                settle(ref, sem)

    barrier = pltpu.get_barrier_semaphore()

    @pl.loop(1, NR)
    def _(j):
        pl.semaphore_signal(barrier, inc=1, device_id={"row": row_peer(j)}, device_id_type=MESH)

    @pl.loop(1, NC)
    def _(j):
        pl.semaphore_signal(barrier, inc=1, device_id={"col": col_peer(j)}, device_id_type=MESH)

    across = lax.div(r, 2)
    source = z * NX + x
    takes = lax.div(x, 2) == k
    half = lax.rem(x, 2)

    @pl.when(takes)
    def _():
        @pl.loop(0, NC)
        def _(p):
            @pl.when((source != r) | (p != c))
            def _():
                pl.semaphore_signal(
                    barrier, inc=1, device_id={"row": source, "col": p}, device_id_type=MESH
                )

    own_target = across == c

    block = 32

    @pl.loop(0, 256 // block)
    def _(b):
        ids = lax.broadcasted_iota(jnp.int32, (block, 256), 0) + b * block
        total = jnp.zeros((block, 256), F32)
        for n in range(32):
            total += jnp.where(ids == nbr_ref[n : n + 1, :], sw_ref[n : n + 1, :], 0.0)
        select[pl.ds(b * block, block), :] = total

    kinds = lax.broadcasted_iota(jnp.int32, (4, 256), 0)
    onehot = (kinds == types_ref[...]).astype(F32)
    mixed = env_ref[...] + dot3(te_ref[...], onehot, COLS)
    descriptor = dot3(mixed, select[...], NORMAL) / math.sqrt(32)
    hidden = jnp.tanh(descriptor)
    activity = jnp.tanh(dot3(hidden, w_ref[...], COLS))
    weighted = dot3(fw_ref[...], activity, NORMAL)
    scale = 1.0 / math.sqrt(256)
    predicted = jnp.sum(weighted * ow_ref[...], axis=1, keepdims=True) * scale
    error = tgt_ref[...] - predicted
    slopes = ow_ref[...] * (1.0 - activity * activity)
    jac = dot3(hidden * fw_ref[...], slopes, NORMAL) * scale

    for n in range(NC):
        jcol_send[n] = jac[4 * n : 4 * n + 4, :]
    for n in range(NR):
        jrow_send[n] = jac[2 * n : 2 * n + 2, :]
    e_send[0] = jnp.broadcast_to(error, (1, 128))
    cov_hi[...], cov_lo[...] = split(cov_ref[...])
    at = lax.broadcasted_iota(jnp.int32, (512, 512), 0)
    to = lax.broadcasted_iota(jnp.int32, (512, 512), 1)
    order[...] = (to == lax.rem(at, NC) * NR + lax.div(at, NC)).astype(F32).astype(BF16)

    pl.semaphore_wait(barrier, NR - 1 + NC - 1 + NY - own_target.astype(jnp.int32))

    zs = [lax.rem(z + d, NZ) * 2 for d in range(NZ)]
    ys = [lax.rem(y + d, NY) for d in range(NY)]
    xs = [lax.rem(x + d, NX) for d in range(NX)]
    for dz, dk in far_first(NZ, 2):
        p = zs[dz] + (k if dk == 0 else 1 - k)
        push("jcol", jcol_send.at[p], jc_recv.at[c], col=p)

    @pl.loop(1, NR)
    def _(j):
        p = row_peer(j)
        push("jrow", jrow_send.at[p], jr_recv.at[r], row=p)

    @pl.loop(1, NC)
    def _(j):
        push("err", e_send.at[0], e_recv.at[c], col=col_peer(j))

    track("jcol", jcol_send.at[pl.ds(0, NC - 1)], jc_recv.at[pl.ds(0, NC - 1)])
    track("jrow", jrow_send.at[pl.ds(0, NR - 1)], jr_recv.at[pl.ds(0, NR - 1)])
    track("err", e_recv.at[pl.ds(0, NC - 1)], e_recv.at[pl.ds(0, NC - 1)])
    jc_recv[c] = jcol_send[c]
    jr_recv[r] = jrow_send[r]
    e_recv[c] = e_send[0]

    land("jcol")
    jc_all[r] = jnp.concatenate([jc_recv[:, n, :] for n in range(4)], axis=1)

    for j in NEAR:
        push("jc_y", jc_all.at[r], jc_all.at[r], jc_y.at[j], row=y_peer(j))
    for i in (1, 3, 2):
        push("jc_x", jc_all.at[r], jc_all.at[r], jc_x.at[0], row=x_peer(i))
    track("jc_y", jc_all.at[pl.ds(0, NY - 1)])
    track("jc_x", jc_all.at[pl.ds(0, NR - NY)])

    land("jrow")
    jr_all[z, k] = jnp.concatenate([jr_recv[:, n, :] for n in range(2)], axis=1)
    for j in NEAR:
        push("jr_z", jr_all.at[z, k], jr_all.at[z, k], col=z_peer(j))
    track("jr_z", jr_all.at[pl.ds(0, NZ - 1), 0], jr_all.at[pl.ds(0, NZ - 1), 0])

    def pass_jc(j):
        slot = y_peer(NY - j)
        settle(jc_all.at[slot], jc_y.at[j])
        for i in (1, 3, 2):
            push("jc_x", jc_all.at[slot], jc_all.at[slot], jc_x.at[j], row=x_peer(i))

    cov = (cov_hi[...], cov_lo[...])
    for j in NEAR[:3]:
        pass_jc(j)
    for n, j in enumerate((0,) + NEAR):
        there = lax.rem(y + NY - j, NY)
        settle(jc_all.at[pl.ds(0, NX - 1)], jc_x.at[j])
        part = dot3(jc_all[pl.ds(there * NX, NX)].reshape(64, 512), cov, ROWS)
        w_send[there] = part.reshape(2, NR, 256)
        for h in range(2):

            @pl.when(2 * there + h != c)
            def _():
                push("w", w_send.at[there, h], w_recv.at[c], col=2 * there + h)

            @pl.when(2 * there + h == c)
            def _():
                w_recv[c] = w_send[there, h]

        if n + 3 < len(NEAR):
            pass_jc(NEAR[n + 3])
        if n == 5:
            land("jr_z")
            push("jr_p", jr_all.at[:, k], jr_all.at[:, k], col=partner)
            track("jr_p", jr_all.at[:, 0], jr_all.at[:, 0])
    track("w", w_recv.at[pl.ds(0, NC - 1)], w_recv.at[pl.ds(0, NC - 1)])

    land("err")
    lanes = lax.broadcasted_iota(jnp.int32, (NC, 128), 1)
    spots = lax.broadcasted_iota(jnp.int32, (NC, 128), 0)
    e_all[r] = jnp.sum(jnp.where(lanes == spots, e_recv[:, 0, :], 0.0), axis=0, keepdims=True)

    land("jr_p")
    jh, jl = split(jr_all[...].reshape(512, 256))
    perm = order[...]
    jr = (mm(perm, jh, NORMAL).astype(BF16), mm(perm, jl, NORMAL).astype(BF16))

    land("w")
    own = jnp.sum(w_recv[...], axis=0)
    art[z, k] = own

    s_part = dot3(own, jr, ROWS)
    for n in range(4):
        s_send[:, n, :] = s_part[:, 128 * n : 128 * n + 128]

    for dy, dx in far_first(NY, NX):
        push("s", s_send.at[xs[dx] * NY + ys[dy]], s_recv.at[r], row=ys[dy] * NX + xs[dx])

    track("s", s_send.at[pl.ds(0, NR - 1)], s_recv.at[pl.ds(0, NR - 1)])
    s_recv[r] = s_send[x * NY + y]

    for j in (0,) + NEAR:
        to_row = y_peer(j)
        if j == 0:

            @pl.when(jnp.logical_not(own_target))
            def _():
                push("act", art.at[z, k], act.at[half, c], act_in.at[c], row=to_row, col=across)

            @pl.when(own_target)
            def _():
                act[half, c] = own

        else:
            push("act", art.at[z, k], act.at[half, c], act_in.at[c], row=to_row, col=across)
    track("act", art.at[pl.ds(0, NY - 1), 0])

    land("s")
    spot = z * NY + y
    s_rows[spot] = jnp.sum(s_recv[...], axis=0)

    for dy, dz in far_first(NY, NZ):
        push("s_yz", s_rows.at[spot], s_rows.at[spot], row=ys[dy] * NX + x, col=zs[dz] + k)

    most = s_rows.at[pl.ds(0, NY * NZ - 1)]
    track("s_yz", most, most)

    for j in NEAR:
        push("art_z", art.at[z, k], art.at[z, k], col=z_peer(j))
    track("art_z", art.at[pl.ds(0, NZ - 1), 0], art.at[pl.ds(0, NZ - 1), 0])

    @pl.when(takes)
    def _():
        for j in (0, 1, 7, 2, 6, 3, 5, 4):
            for h in range(2):
                p = lax.rem(z + j, NZ) * 2 + h

                @pl.when((source != r) | (p != c))
                def _():
                    settle(act.at[half, p], act_in.at[p])

                for i in (1, 3, 2):
                    push("act_x", act.at[half, p], act.at[half, p], act_x.at[half], row=x_peer(i))

    @pl.loop(1, NR)
    def _(j):
        push("e", e_all.at[r], e_all.at[r], row=row_peer(j))

    track("e", e_all.at[pl.ds(0, NR - 1)], e_all.at[pl.ds(0, NR - 1)])

    land("s_yz")
    for n in range(NZ):
        s_all[n, k, x] = jnp.concatenate([s_rows[NY * n : NY * n + NY, i, :] for i in range(4)], axis=1)
    for i in (1, 3, 2):
        push("s_x", s_all.at[:, k, x], s_all.at[:, k, x], s_g.at[i], row=x_peer(i))
    track("s_x", s_all.at[:, 0, pl.ds(0, NX - 1)])
    push("s_p", s_all.at[:, k, x], s_all.at[:, k, x], col=partner)
    land("art_z")
    push("art_p", art.at[:, k], art.at[:, k], col=partner)
    track("art_p", art.at[:, 0], art.at[:, 0])
    for i in (1, 3, 2):
        origin = lax.rem(x + NX - i, NX)
        settle(s_all.at[:, k, origin], s_g.at[i])
        push("s_p", s_all.at[:, k, origin], s_all.at[:, k, origin], col=partner)
    track("s_p", s_all.at[:, 0], s_all.at[:, 0])

    land("e")
    spread = (
        lax.broadcasted_iota(jnp.int32, (512, NR), 1)
        == lax.div(lax.broadcasted_iota(jnp.int32, (512, NR), 0), NC)
    ).astype(F32)
    errors = jnp.concatenate([e_all[n] for n in range(NR)], axis=0)
    picked = jnp.dot(spread, errors, precision=lax.Precision.HIGHEST)
    own_lane = lax.broadcasted_iota(jnp.int32, (512, 128), 1) == lax.rem(
        lax.broadcasted_iota(jnp.int32, (512, 128), 0), NC
    )
    errors = dot3(jnp.ones((8, 128), F32), jnp.where(own_lane, picked, 0.0), ROWS)
    land("art_p")
    products = art[...].reshape(512, 256).T
    land("s_p")

    eye = at == to
    innovation = s_all[...].reshape(512, 512) + jnp.where(eye, FORGET, 0.0)
    bound = jnp.max(jnp.sum(jnp.abs(innovation), axis=0, keepdims=True), axis=1, keepdims=True)
    ph, pw = split(jnp.where(eye, 1.0, 0.0) - innovation / bound)
    gain = products / bound
    for step in range(2):
        gh, gl = split(gain)
        first = mm(jnp.concatenate([ph, gh, gl], axis=0), ph, NORMAL)
        second = mm(jnp.concatenate([ph, gh], axis=0), pw, NORMAL)
        mixed = second[:512]
        gain = gain + (first[512:768] + (first[768:] + second[512:]))
        ph, pw = split(first[:512] + (mixed + mixed.T))
    power = (ph, pw)
    gain = gain + dot3(gain, power, NORMAL)
    gain = gain + dot3(dot3(gain, power, NORMAL), power, NORMAL)
    gain_ref[...] = gain

    delta = dot3(errors, gain, ROWS)[:1]
    upper = lax.div(c, 8)
    delta = jnp.where(upper == 0, delta[:, :128], delta[:, 128:])
    moved = w_ref[pl.ds(2 * r + upper, 1), :] + delta
    moved = pltpu.roll(moved, 128 - 16 * lax.rem(c, 8), 1)
    weight_ref[...] = moved[:, :16]

    for h in range(2):

        @pl.when(jnp.logical_not(takes & (half == h)))
        def _():
            settle(act.at[h], act_x.at[h])

    @pl.when(jnp.logical_not(own_target))
    def _():
        settle(art.at[0, 0], send.at[GROUPS.index("act")])

    @pl.when(takes)
    def _():
        for i in range(3):
            settle(act.at[0], send.at[GROUPS.index("act_x")])

    drain()


def finish(gain_ref, act_ref, cov_ref, weight_ref, newcov_ref, new_weight_ref):
    update = dot3(gain_ref[...], act_ref[pl.program_id(0)], NORMAL)
    newcov_ref[...] = (cov_ref[...] - update) * (1.0 / FORGET)
    new_weight_ref[...] = weight_ref[...]


def on_device(
    atom_types, neighbor_ids, switching, environment, force_weights, targets,
    type_embed, layer_weight, out_weight, covariance,
):
    vmem = pl.BlockSpec(memory_space=pltpu.VMEM)
    V = pltpu.VMEM
    D = pltpu.SemaphoreType.DMA
    scratch = [
        V((256, 256), F32), V((256, 512), BF16), V((256, 512), BF16), V((512, 512), BF16),
        V((NR, 2, 128), F32), V((NC, 4, 128), F32), V((1, 1, 128), F32),
        V((NR, 2, 128), F32), V((NC, 4, 128), F32), V((NC, 1, 128), F32), V((NR, 1, 128), F32),
        V((NZ, 2, NR, 256), F32), V((NR, NC, 512), F32),
        V((NY, 2, NR, 256), F32), V((NC, NR, 256), F32), V((NZ, 2, NR, 256), F32),
        V((NR, 4, 128), F32), V((NR, 4, 128), F32), V((NZ * NY, 4, 128), F32), V((NZ, 2, NX, 8, 512), F32),
        D((len(GROUPS),)), D((len(GROUPS),)), D((NY,)), D((NY,)), D((NC,)), D((2,)), D((NX,)),
    ]
    gain, act, weight = pl.pallas_call(
        kernel,
        out_shape=(
            V((256, 512), F32),
            V((2, NC, NR, 256), F32),
            jax.ShapeDtypeStruct((1, 16), F32),
        ),
        in_specs=[vmem] * 10,
        out_specs=(vmem, vmem, vmem),
        scratch_shapes=scratch,
        compiler_params=pltpu.CompilerParams(
            collective_id=0, has_side_effects=True, vmem_limit_bytes=60 * 1024 * 1024
        ),
    )(
        atom_types, neighbor_ids[0], switching[0], environment[0].T, force_weights,
        targets.reshape(1, 1), type_embed, layer_weight, out_weight.reshape(1, 128), covariance,
    )
    keep = functools.partial(pltpu.with_memory_space_constraint, memory_space=pltpu.VMEM)
    new_cov, new_weight = pl.pallas_call(
        finish,
        grid=(2,),
        out_shape=(
            jax.ShapeDtypeStruct((256, 512), F32),
            jax.ShapeDtypeStruct((1, 16), F32),
        ),
        in_specs=[
            vmem,
            vmem,
            pl.BlockSpec((256, 256), lambda h: (0, h)),
            pl.BlockSpec((1, 16), lambda h: (0, 0)),
        ],
        out_specs=(
            pl.BlockSpec((256, 256), lambda h: (0, h)),
            pl.BlockSpec((1, 16), lambda h: (0, 0)),
        ),
    )(keep(gain), keep(act.reshape(2, 512, 256)), covariance, weight)
    return (new_weight.reshape(16), new_cov)


def solution(mesh):
    in_specs = (
        P(("row", "col"), None),
        P(("row", "col"), None, None),
        P(("row", "col"), None, None),
        P(("row", "col"), None, None),
        P(("row", "col"), None),
        P(("row", "col")),
        P(),
        P(),
        P(),
        P("row", "col"),
    )
    out_specs = (P(("row", "col")), P("row", "col"))
    return jax.shard_map(
        on_device, mesh=mesh, in_specs=in_specs, out_specs=out_specs, check_vma=False
    )
```
